128 devices in a mesh: order: 2 (over core), tok: 64 (over z, y, x).
Axes of the slice: x: 4, y: 4, z: 4, core: 2. Of those that a mesh axis runs over, the one named last changes fastest.
Arguments:
- queries: bfloat16 [262144, 512], P(('order', 'tok')), may hold values from -6 to 6
- key_tokens: bfloat16 [262144, 512], P(('order', 'tok')), may hold values from -6 to 6
- value_tokens: bfloat16 [262144, 512], P(('order', 'tok')), may hold values from -6 to 6
- learn_rates: float32 [262144], P(('order', 'tok')), may hold values from 0.02 to 0.2
- fast_init: float32 [512, 1536], replicated, may hold values from -0.25 to 0.25
- out_gain: float32 [512], replicated, may hold values from 0.5 to 1.5
Outputs:
- output: bfloat16 [262144, 512], P(('order', 'tok'))
The draws below stay inside these ranges and needn't reach their ends.
All inputs are finite; a program needn't handle non-finite values.
Results may differ from the reference program's by a relative error of at most 0.015.
Values may be sent and summed in bfloat16 or wider, within the bound.
No kernel may reach another device: no remote copies, remote signals or barrier semaphores. Data moves between devices by JAX's collectives and lax.ppermute only.
A program may use at most 128 MiB of HBM per device.

```python
import math
import jax
import jax.numpy as jnp
from jax import lax

D = 512
TOK_DEV = 2048
TOKENS = 262144
N_ORDER = 2
N_TOK = 64


def block_scale(stream_key, dims, split, smallest, largest):
    level = 1.0
    for position, shards_of in split:
        heights = jax.random.uniform(jax.random.fold_in(jax.random.fold_in(stream_key, 6), position), (shards_of,), jnp.float32, smallest / len(split), largest / len(split))
        level = level * jnp.repeat(jnp.exp(heights), dims[position] // shards_of).reshape((-1,) + (1,) * (len(dims) - 1 - position))
    return level


def normal_values(key, shape, scale, bound, split=(), kind=jnp.bfloat16):
    values = scale * jax.random.normal(key, shape, jnp.float32)
    if split:
        values = values * block_scale(key, shape, split, -0.22, 0.18)
    return jnp.clip(values, -bound, bound).astype(kind)


def setup_inputs(seed: int = 0) -> dict:
    streams_of = jax.random.split(jax.random.key(seed), 7)
    queries = normal_values(streams_of[0], (TOKENS, D), 1.0, 6.0, ((0, 128),))
    key_tokens = normal_values(streams_of[1], (TOKENS, D), 1.0, 6.0, ((0, 128),))
    value_tokens = normal_values(streams_of[2], (TOKENS, D), 1.0, 6.0, ((0, 128),))
    learn_rates = jnp.clip(jnp.exp(math.log(0.2) - 2.3025851 * jax.random.uniform(streams_of[3], (TOKENS,), jnp.float32) ** block_scale(streams_of[3], (TOKENS,), ((0, 128),), -0.2, 0.2)), 0.02, 0.2)
    fast_init = normal_values(streams_of[4], (D, 3 * D), D ** -0.5, 0.25, (), jnp.float32)
    out_gain = jnp.clip(1.0 + 0.1 * jax.random.normal(streams_of[5], (D,), jnp.float32), 0.5, 1.5)
    return {"queries": queries, "key_tokens": key_tokens, "value_tokens": value_tokens, "learn_rates": learn_rates, "fast_init": fast_init, "out_gain": out_gain}


def gate_up(rows_in, weights_bf):
    width = weights_bf.shape[0]
    both_parts = jnp.dot(rows_in, weights_bf[:, :2 * width], preferred_element_type=jnp.float32)
    return (both_parts[:, :width], both_parts[:, width:])

def gradient(key_rows, target, weights):
    width = weights.shape[0]
    weights_bf = weights.astype(jnp.bfloat16)
    gate_pre, up_pre = gate_up(key_rows, weights_bf)
    squash = jax.nn.sigmoid(gate_pre)
    activated = gate_pre * squash
    hidden = (activated * up_pre).astype(jnp.bfloat16)
    hidden_grad = lax.dot_general(target, weights_bf[:, 2 * width:], (((1,), (1,)), ((), ())), preferred_element_type=jnp.float32)
    gate_grad = (hidden_grad * up_pre * squash * (1.0 + gate_pre * (1.0 - squash))).astype(jnp.bfloat16)
    up_grad = (hidden_grad * activated).astype(jnp.bfloat16)
    inner_grads = jnp.concatenate([gate_grad, up_grad], axis=1)
    upper = lax.dot_general(key_rows, inner_grads, (((0,), (0,)), ((), ())), preferred_element_type=jnp.float32)
    lower = lax.dot_general(hidden, target, (((0,), (0,)), ((), ())), preferred_element_type=jnp.float32)
    return jnp.concatenate([upper, lower], axis=1)

def apply_weights(query_rows, closing, out_gain):
    width = closing.shape[0]
    weights_bf = closing.astype(jnp.bfloat16)
    gate_pre, up_pre = gate_up(query_rows, weights_bf)
    hidden = (jax.nn.silu(gate_pre) * up_pre).astype(jnp.bfloat16)
    result = jnp.dot(hidden, weights_bf[:, 2 * width:], preferred_element_type=jnp.float32)
    norm_inv = lax.rsqrt(lax.optimization_barrier(jnp.mean(result * result, axis=1, keepdims=True)) + 1e-06)
    return (result * norm_inv * out_gain[None, :]).astype(jnp.bfloat16)

def reference(queries, key_tokens, value_tokens, learn_rates, fast_init, out_gain):
    group_rows = TOK_DEV * N_TOK
    factor = group_rows ** (-0.5)
    changes = []
    for group_index in range(N_ORDER):
        low = group_index * group_rows
        key_rows = key_tokens[low:low + group_rows]
        target = (-(learn_rates[low:low + group_rows, None] * factor) * value_tokens[low:low + group_rows].astype(jnp.float32)).astype(jnp.bfloat16)
        first_step = fast_init - gradient(key_rows, target, fast_init)
        second_step = first_step - gradient(key_rows, target, first_step)
        changes.append(second_step - fast_init)
    outputs = []
    earlier = jnp.zeros_like(fast_init)
    for group_index in range(N_ORDER):
        low = group_index * group_rows
        closing = fast_init + earlier + changes[group_index]
        outputs.append(apply_weights(queries[low:low + group_rows], closing, out_gain))
        earlier = earlier + changes[group_index]
    return jnp.concatenate(outputs, axis=0)
```

```python
import functools
import itertools

import jax
import jax.numpy as jnp
from jax import lax
from jax.experimental import pallas as pl
from jax.experimental.pallas import tpu as pltpu
from jax.sharding import PartitionSpec as P

SIDE = 4
AXES = ("order", "tok")
BF = jnp.bfloat16
F32 = jnp.float32
NT = (((1,), (1,)), ((), ()))
NN = (((1,), (0,)), ((), ()))
VMEM = pl.BlockSpec(memory_space=pltpu.VMEM)
SMEM = pl.BlockSpec(memory_space=pltpu.SMEM)


def flat(core, z, y, x):
    return ((core * SIDE + z % SIDE) * SIDE + y % SIDE) * SIDE + x % SIDE


def hop_pairs(level, step):
    pairs = []
    for core, z, y, x in itertools.product(range(2), *[range(SIDE)] * 3):
        dz = dy = dx = 0
        if level == 2:
            dz = step
        elif (level == 0) == (core == 0):
            dx = step
        else:
            dy = step
        pairs.append((flat(core, z, y, x), flat(core, z + dz, y + dy, x + dx)))
    return pairs


def hop(x, level, step):
    return lax.ppermute(x, AXES, hop_pairs(level, step % SIDE))


def call(kernel, outs, n_smem, args, cost, scratch=(), limit=24 << 20):
    return pl.pallas_call(
        kernel,
        out_shape=outs,
        in_specs=[SMEM] * n_smem + [VMEM] * (len(args) - n_smem),
        out_specs=jax.tree.map(lambda _: VMEM, outs),
        scratch_shapes=scratch,
        compiler_params=pltpu.CompilerParams(vmem_limit_bytes=limit),
        cost_estimate=pl.CostEstimate(flops=cost[0], bytes_accessed=cost[1], transcendentals=0),
    )(*args)


def arr(shape, dtype):
    return jax.ShapeDtypeStruct(shape, dtype)


def layout_kernel(place, w_ref, b0, b1, b2, b3, own, turned, slab):
    width = w_ref.shape[0]
    lines = width // (SIDE * SIDE)
    for m in range(2):
        part = w_ref[:, m * width : (m + 1) * width].astype(BF)
        turned[m] = part.T.reshape(SIDE * SIDE, lines, width)
    turned[2] = w_ref[:, 2 * width :].astype(BF).reshape(SIDE * SIDE, lines, width)
    for r, block in enumerate((b0, b1, b2, b3)):
        for s in range(SIDE):
            group = place[r * SIDE + s]
            for m in range(3):
                block[s, m] = turned[m, group]
    mine = place[0]
    for m in range(2):
        start = pl.multiple_of(m * width + (mine // SIDE) * 128, 128)
        slab[...] = w_ref[:, pl.ds(start, 128)].T.reshape(SIDE, lines, width)
        own[m] = slab[mine % SIDE]
    own[2] = w_ref[pl.ds(pl.multiple_of(mine * lines, lines), lines), 2 * width :]


def gradient_kernel(factor, tile, w_ref, k_ref, v_ref, rate_ref, out_ref, acc):
    units = w_ref.shape[0] * w_ref.shape[2]
    width = w_ref.shape[3]
    lines = w_ref.shape[2]
    wgu = jnp.concatenate([w_ref[:, m].reshape(units, width) for m in range(2)], axis=0)
    wd = w_ref[:, 2].reshape(units, width)
    tokens = k_ref.shape[0]

    def one(i, first):
        rows = pl.ds(i * tile, tile) if first else pl.ds(pl.multiple_of(i * tile, tile), tile)
        k = k_ref[rows, :]
        v = v_ref[rows, :]
        scale = -(rate_ref[:, rows] * factor)
        gu = lax.dot_general(wgu, k, NT, preferred_element_type=F32)
        hidden_grad = lax.dot_general(wd, v, NT, preferred_element_type=F32) * scale
        gate = gu[:units]
        up = gu[units:]
        sig = 0.5 * jnp.tanh(0.5 * gate) + 0.5
        act = gate * sig
        hidden = (act * up * scale).astype(BF)
        gate_grad = (hidden_grad * up * (sig + act * (1.0 - sig))).astype(BF)
        up_grad = (hidden_grad * act).astype(BF)
        both = jnp.concatenate([gate_grad, up_grad], axis=0)
        upper = lax.dot_general(both, k, NN, preferred_element_type=F32)
        lower = lax.dot_general(hidden, v, NN, preferred_element_type=F32)
        if first:
            acc[: 2 * units] = upper
            acc[2 * units :] = lower
        else:
            acc[: 2 * units] += upper
            acc[2 * units :] += lower

    one(0, True)

    @pl.loop(1, tokens // tile)
    def _(i):
        one(i, False)

    for m in range(3):
        part = acc[m * units : (m + 1) * units]
        out_ref[:, m] = part.reshape(SIDE, lines, width).astype(out_ref.dtype)


def gradient_block(weights, keys, values, rates, factor, dtype, tile=512):
    units = weights.shape[0] * weights.shape[2]
    width = weights.shape[3]
    tokens = keys.shape[0]
    return call(
        functools.partial(gradient_kernel, factor, tile),
        arr(weights.shape, dtype),
        0,
        (weights, keys, values, rates),
        (12 * tokens * width * units, 4 * tokens * width),
        [pltpu.VMEM((3 * units, width), F32)],
    )


def scatter_kernel(own, r1, r2, r3, keep, s1, s2, s3):
    for s, out in enumerate((keep, s1, s2, s3)):
        total = own[s] + r1[s].astype(F32) + r2[s].astype(F32) + r3[s].astype(F32)
        out[...] = total.astype(out.dtype)


def add_kernel(own, r1, r2, r3, out):
    out[...] = (
        own[...] + r1[...].astype(F32) + r2[...].astype(F32) + r3[...].astype(F32)
    ).astype(out.dtype)


def update_kernel(weights, own, r1, r2, r3, new, new_bf):
    total = (
        own[...].astype(F32) + r1[...].astype(F32) + r2[...].astype(F32) + r3[...].astype(F32)
    )
    value = weights[...] - total
    new[...] = value
    new_bf[...] = value.astype(BF)


def change_kernel(start, weights, own, r1, r2, r3, change, change_bf):
    total = (
        own[...].astype(F32) + r1[...].astype(F32) + r2[...].astype(F32) + r3[...].astype(F32)
    )
    value = (weights[...] - total) - start[...]
    change[...] = value
    change_bf[...] = value.astype(BF)


def closing_kernel(start, earlier, change, out):
    out[...] = ((start[...] + earlier[...].astype(F32)) + change[...]).astype(BF)


def join_kernel(own, r1, r2, r3, out):
    for s, part in enumerate((own, r1, r2, r3)):
        out[s] = part[...]


def apply_kernel(tile, first, last, *refs):
    refs = list(refs)
    w_ref, q_ref = refs[:2]
    refs = refs[2:]
    gain = refs.pop(0) if last else None
    so_far = None if first else refs.pop(0)
    out = refs.pop(0)
    units = w_ref.shape[0] * w_ref.shape[2]
    width = w_ref.shape[3]
    wgu = jnp.concatenate([w_ref[:, m].reshape(units, width) for m in range(2)], axis=0)
    wd = w_ref[:, 2].reshape(units, width)

    @pl.loop(0, q_ref.shape[0] // tile)
    def _(i):
        rows = pl.ds(pl.multiple_of(i * tile, tile), tile)
        gu = lax.dot_general(q_ref[rows, :], wgu, NT, preferred_element_type=F32)
        gate = gu[:, :units]
        up = gu[:, units:]
        act = gate * (0.5 * jnp.tanh(0.5 * gate) + 0.5)
        y = lax.dot_general((act * up).astype(BF), wd, NN, preferred_element_type=F32)
        if so_far is not None:
            y = y + so_far[rows, :]
        if last:
            scale = lax.rsqrt(jnp.mean(y * y, axis=1, keepdims=True) + 1e-06)
            y = y * scale * gain[...]
        out[rows, :] = y.astype(out.dtype)


def apply_block(weights, queries, so_far, gain, tile=512):
    units = weights.shape[0] * weights.shape[2]
    tokens, width = queries.shape
    first, last = so_far is None, gain is not None
    args = (weights, queries) + ((gain,) if last else ()) + (() if first else (so_far,))
    return call(
        functools.partial(apply_kernel, tile, first, last),
        arr((tokens, width), BF if last else F32),
        0,
        args,
        (6 * tokens * width * units, 6 * tokens * width),
    )


def ring_parts(x, level):
    return [hop(x, level, -r) for r in range(1, SIDE)]


def total_parts(blocks, keys, values, rates, factor):
    sent = {}
    for r in (2, 1, 3):
        sent[r] = hop(gradient_block(blocks[r], keys, values, rates, factor, BF), 0, r)
    own = gradient_block(blocks[0], keys, values, rates, factor, F32)
    shard = own.shape[1:]
    size = own.size
    keep, *out = call(
        scatter_kernel,
        [arr(shard, F32)] + [arr(shard, BF)] * 3,
        0,
        (own, sent[1], sent[2], sent[3]),
        (3 * size, 12 * size),
    )
    got = [hop(x, 1, r + 1) for r, x in enumerate(out)]
    part = call(add_kernel, arr(shard, BF), 0, (keep, *got), (size, 3 * size))
    return [part] + ring_parts(part, 2)


def gathered(shard):
    parts = [shard] + ring_parts(shard, 1)
    block = call(join_kernel, arr((SIDE, *shard.shape), BF), 0, parts, (0, 16 * shard.size))
    return [block] + ring_parts(block, 0)


def shards(queries, key_tokens, value_tokens, learn_rates, fast_init, out_gain):
    tokens, width = key_tokens.shape
    factor = (tokens * lax.axis_size("tok")) ** (-0.5)
    lines = width // (SIDE * SIDE)
    core = lax.axis_index("order")
    tok = lax.axis_index("tok")
    x, y = tok % SIDE, (tok // SIDE) % SIDE
    ring = jnp.arange(SIDE, dtype=jnp.int32)
    r1, r2 = ring[:, None], ring[None, :]
    along_x = (x + jnp.where(core == 0, r1, r2)) % SIDE
    along_y = (y + jnp.where(core == 0, r2, r1)) % SIDE
    place = (along_x * SIDE + along_y).reshape(-1).astype(jnp.int32)
    rates = learn_rates.reshape(1, tokens)
    gain = out_gain.reshape(1, width)

    shard = (3, lines, width)
    *blocks, start = call(
        layout_kernel,
        [arr((SIDE, *shard), BF)] * SIDE + [arr(shard, F32)],
        1,
        (place, fast_init),
        (0, 6 * fast_init.size),
        [
            pltpu.VMEM((3, SIDE * SIDE, lines, width), BF),
            pltpu.VMEM((SIDE, lines, width), F32),
        ],
    )
    size = start.size
    parts = total_parts(blocks, key_tokens, value_tokens, rates, factor)
    first_step, first_bf = call(
        update_kernel, [arr(shard, F32), arr(shard, BF)], 0, (start, *parts), (size, 8 * size)
    )
    blocks = gathered(first_bf)
    parts = total_parts(blocks, key_tokens, value_tokens, rates, factor)
    change, change_bf = call(
        change_kernel,
        [arr(shard, F32), arr(shard, BF)],
        0,
        (start, first_step, *parts),
        (size, 8 * size),
    )
    pairs = [(flat(0, *c), flat(1, *c)) for c in itertools.product(*[range(SIDE)] * 3)]
    earlier = lax.ppermute(change_bf, AXES, pairs)
    closing = call(closing_kernel, arr(shard, BF), 0, (start, earlier, change), (size, 8 * size))
    blocks = gathered(closing)
    result = apply_block(blocks[0], queries, None, None)
    for r in (1, 3):
        result = apply_block(blocks[r], queries, result, None)
    return apply_block(blocks[2], queries, result, gain)


def solution(mesh):
    rows = P(AXES, None)
    return jax.shard_map(
        shards,
        mesh=mesh,
        in_specs=(rows, rows, rows, P(AXES), P(), P()),
        out_specs=rows,
        check_vma=False,
    )
```

```python
import functools
import itertools

import jax
import jax.numpy as jnp
from jax import lax
from jax.experimental import pallas as pl
from jax.experimental.pallas import tpu as pltpu
from jax.sharding import PartitionSpec as P

SIDE = 4
AXES = ("order", "tok")
BF = jnp.bfloat16
F32 = jnp.float32
NT = (((1,), (1,)), ((), ()))
NN = (((1,), (0,)), ((), ()))
VMEM = pl.BlockSpec(memory_space=pltpu.VMEM)
SMEM = pl.BlockSpec(memory_space=pltpu.SMEM)


def flat(core, z, y, x):
    return ((core * SIDE + z % SIDE) * SIDE + y % SIDE) * SIDE + x % SIDE


def hop_pairs(level, step):
    pairs = []
    for core, z, y, x in itertools.product(range(2), *[range(SIDE)] * 3):
        dz = dy = dx = 0
        if level == 2:
            dz = step
        elif (level == 0) == (core == 0):
            dx = step
        else:
            dy = step
        pairs.append((flat(core, z, y, x), flat(core, z + dz, y + dy, x + dx)))
    return pairs


def hop(x, level, step):
    return lax.ppermute(x, AXES, hop_pairs(level, step % SIDE))


HBM = pl.BlockSpec(memory_space=pltpu.HBM)


def call(kernel, outs, specs, args, cost, scratch=(), out_spec=VMEM, limit=24 << 20):
    return pl.pallas_call(
        kernel,
        out_shape=outs,
        in_specs=specs or [VMEM] * len(args),
        out_specs=jax.tree.map(lambda _: out_spec, outs),
        scratch_shapes=scratch,
        compiler_params=pltpu.CompilerParams(vmem_limit_bytes=limit),
        cost_estimate=pl.CostEstimate(flops=cost[0], bytes_accessed=cost[1], transcendentals=0),
    )(*args)


def arr(shape, dtype):
    return jax.ShapeDtypeStruct(shape, dtype)


def first_kernel(factor, tile, place, *refs):
    sources, (b0, b2, own, g1, g3), scratch = refs[:4], refs[4:9], refs[9:]
    w_ref, k_ref, v_ref, rate_ref, turned, slab, b1, b3, grads, hiddens, sems = scratch
    copies = [
        pltpu.make_async_copy(src, dst, sems.at[i])
        for i, (src, dst) in enumerate(zip(sources, scratch[:4]))
    ]
    for copy in copies:
        copy.start()
    copies[0].wait()
    width = w_ref.shape[0]
    lines = width // (SIDE * SIDE)
    for m in range(2):
        part = w_ref[:, m * width : (m + 1) * width].astype(BF)
        turned[m] = part.T.reshape(SIDE * SIDE, lines, width)
    turned[2] = w_ref[:, 2 * width :].astype(BF).reshape(SIDE * SIDE, lines, width)
    for r, block in enumerate((b0, b1, b2, b3)):
        for s in range(SIDE):
            group = place[r * SIDE + s]
            for m in range(3):
                block[s, m] = turned[m, group]
    mine = place[0]
    for m in range(2):
        start = pl.multiple_of(m * width + (mine // SIDE) * 128, 128)
        slab[...] = w_ref[:, pl.ds(start, 128)].T.reshape(SIDE, lines, width)
        own[m] = slab[mine % SIDE]
    own[2] = w_ref[pl.ds(pl.multiple_of(mine * lines, lines), lines), 2 * width :]
    for copy in copies[1:]:
        copy.wait()
    gradient_kernel(factor, tile, 2, b1, b3, k_ref, v_ref, rate_ref, g1, g3, grads, hiddens)


def rows_of(w_refs, m):
    parts = [w[:, m].reshape(-1, w.shape[3]) for w in w_refs]
    return parts[0] if len(parts) == 1 else jnp.concatenate(parts, axis=0)


def gradient_kernel(factor, tile, count, *refs):
    w_refs, (k_ref, v_ref, rate_ref) = refs[:count], refs[count : count + 3]
    outs, (grads, hiddens) = refs[count + 3 : 2 * count + 3], refs[2 * count + 3 :]
    wgu = jnp.concatenate([rows_of(w_refs, 0), rows_of(w_refs, 1)], axis=0)
    wd = rows_of(w_refs, 2)
    units, width = wd.shape
    for i in range(k_ref.shape[0] // tile):
        rows = slice(i * tile, (i + 1) * tile)
        scale = -(rate_ref[:, rows] * factor)
        gu = lax.dot_general(wgu, k_ref[rows, :], NT, preferred_element_type=F32)
        hidden_grad = lax.dot_general(wd, v_ref[rows, :], NT, preferred_element_type=F32) * scale
        gate = gu[:units]
        up = gu[units:]
        sig = 0.5 * jnp.tanh(0.5 * gate) + 0.5
        act = gate * sig
        hiddens[:, rows] = (act * up * scale).astype(BF)
        grads[:units, rows] = (hidden_grad * up * (sig + act * (1.0 - sig))).astype(BF)
        grads[units:, rows] = (hidden_grad * act).astype(BF)
    upper = lax.dot_general(grads[...], k_ref[...], NN, preferred_element_type=F32)
    lower = lax.dot_general(hiddens[...], v_ref[...], NN, preferred_element_type=F32)
    lines = outs[0].shape[2]
    per = units // count
    for b, out in enumerate(outs):
        own = slice(b * per, (b + 1) * per)
        for m, part in enumerate((upper[:units], upper[units:], lower)):
            out[:, m] = part[own].reshape(SIDE, lines, width).astype(out.dtype)


def gradient_blocks(weights, keys, values, rates, factor, dtype, tile=256):
    count = len(weights)
    units = count * weights[0].shape[0] * weights[0].shape[2]
    tokens, width = keys.shape
    return call(
        functools.partial(gradient_kernel, factor, tile, count),
        [arr(w.shape, dtype) for w in weights],
        None,
        (*weights, keys, values, rates),
        (12 * tokens * width * units, 4 * tokens * width),
        [pltpu.VMEM((2 * units, tokens), BF), pltpu.VMEM((units, tokens), BF)],
    )


def near_kernel(own, r1, r3, out):
    out[...] = own[...] + r1[...].astype(F32) + r3[...].astype(F32)


def scatter_kernel(near, r2, keep, s1, s2, s3):
    for s, out in enumerate((keep, s1, s2, s3)):
        out[...] = (near[s] + r2[s].astype(F32)).astype(out.dtype)


def add_kernel(own, r1, r2, r3, out):
    out[...] = (
        own[...] + r1[...].astype(F32) + r2[...].astype(F32) + r3[...].astype(F32)
    ).astype(out.dtype)


def update_kernel(weights, own, r1, r2, r3, new, new_bf):
    total = (
        own[...].astype(F32) + r1[...].astype(F32) + r2[...].astype(F32) + r3[...].astype(F32)
    )
    value = weights[...] - total
    new[...] = value
    new_bf[...] = value.astype(BF)


def change_kernel(start, weights, own, r1, r2, r3, change, change_bf):
    total = (
        own[...].astype(F32) + r1[...].astype(F32) + r2[...].astype(F32) + r3[...].astype(F32)
    )
    value = (weights[...] - total) - start[...]
    change[...] = value
    change_bf[...] = value.astype(BF)


def closing_kernel(start, earlier, change, out):
    out[...] = ((start[...] + earlier[...].astype(F32)) + change[...]).astype(BF)


def join_kernel(own, r1, r2, r3, out):
    for s, part in enumerate((own, r1, r2, r3)):
        out[s] = part[...]


def apply_kernel(tile, count, first, last, *refs):
    refs = list(refs)
    w_refs, q_ref = refs[:count], refs[count]
    refs = refs[count + 1 :]
    gain = refs.pop(0) if last else None
    so_far = None if first else refs.pop(0)
    out = refs.pop(0)
    wgu = jnp.concatenate([rows_of(w_refs, 0), rows_of(w_refs, 1)], axis=0)
    wd = rows_of(w_refs, 2)
    units = wd.shape[0]
    copies = []
    for i in range(q_ref.shape[0] // tile):
        rows = slice(i * tile, (i + 1) * tile)
        gu = lax.dot_general(q_ref[rows, :], wgu, NT, preferred_element_type=F32)
        gate = gu[:, :units]
        up = gu[:, units:]
        act = gate * (0.5 * jnp.tanh(0.5 * gate) + 0.5)
        y = lax.dot_general((act * up).astype(BF), wd, NN, preferred_element_type=F32)
        if so_far is not None:
            y = y + so_far[rows, :]
        if last:
            held, sems = refs
            scale = lax.rsqrt(jnp.mean(y * y, axis=1, keepdims=True) + 1e-06)
            held[rows, :] = (y * scale * gain[...]).astype(BF)
            copies.append(pltpu.make_async_copy(held.at[rows], out.at[rows], sems.at[i]))
            copies[-1].start()
        else:
            out[rows, :] = y
    for copy in copies:
        copy.wait()


def apply_blocks(weights, queries, so_far, gain, tile=256):
    count = len(weights)
    units = count * weights[0].shape[0] * weights[0].shape[2]
    tokens, width = queries.shape
    first, last = so_far is None, gain is not None
    args = (*weights, queries) + ((gain,) if last else ()) + (() if first else (so_far,))
    scratch = ()
    if last:
        scratch = [pltpu.VMEM((tokens, width), BF), pltpu.SemaphoreType.DMA((tokens // tile,))]
    return call(
        functools.partial(apply_kernel, tile, count, first, last),
        arr((tokens, width), BF if last else F32),
        None,
        args,
        (6 * tokens * width * units, 6 * tokens * width),
        scratch,
        out_spec=HBM if last else VMEM,
    )


def ring_parts(x, level):
    parts = {r: hop(x, level, -r) for r in (1, 3, 2)}
    return [parts[r] for r in range(1, SIDE)]


def in_turn(first, *later):
    return lax.optimization_barrier((first, *later))


def combined(own, sent):
    shard = own.shape[1:]
    size = own.size
    near = call(near_kernel, arr(own.shape, F32), None, (own, sent[1], sent[3]), (2 * size, 8 * size))
    keep, *out = call(
        scatter_kernel,
        [arr(shard, F32)] + [arr(shard, BF)] * 3,
        None,
        (near, sent[2]),
        (size, 8 * size),
    )
    got = {r: hop(out[r - 1], 1, r) for r in (1, 3, 2)}
    part = call(add_kernel, arr(shard, BF), None, (keep, got[1], got[2], got[3]), (size, 3 * size))
    return [part] + ring_parts(part, 2)


def first_totals(place, weights, keys, values, rates, factor, tile=256):
    tokens, width = keys.shape
    lines = width // (SIDE * SIDE)
    block = (SIDE, 3, lines, width)
    units = 2 * SIDE * lines
    b0, b2, start, g1, g3 = call(
        functools.partial(first_kernel, factor, tile),
        [arr(block, BF)] * 2 + [arr(block[1:], F32)] + [arr(block, BF)] * 2,
        [SMEM] + [HBM] * 4,
        (place, weights, keys, values, rates),
        (12 * tokens * width * units, 4 * tokens * width),
        [
            pltpu.VMEM(weights.shape, F32),
            pltpu.VMEM(keys.shape, BF),
            pltpu.VMEM(values.shape, BF),
            pltpu.VMEM(rates.shape, F32),
            pltpu.VMEM((3, SIDE * SIDE, lines, width), BF),
            pltpu.VMEM((SIDE, lines, width), F32),
            pltpu.VMEM(block, BF),
            pltpu.VMEM(block, BF),
            pltpu.VMEM((2 * units, tokens), BF),
            pltpu.VMEM((units, tokens), BF),
            pltpu.SemaphoreType.DMA((4,)),
        ],
        limit=52 << 20,
    )
    sent = {1: hop(g1, 0, 1), 3: hop(g3, 0, 3)}
    (g2,) = gradient_blocks([b2], keys, values, rates, factor, BF)
    sent[2] = hop(g2, 0, 2)
    (own,) = gradient_blocks([b0], keys, values, rates, factor, F32)
    return start, combined(own, sent)


def second_totals(blocks, keys, values, rates, factor):
    sent = {}
    (own,) = gradient_blocks([blocks[0]], keys, values, rates, factor, F32)
    own, keys = in_turn(own, keys)
    g1, g3 = gradient_blocks([blocks[1], blocks[3]], keys, values, rates, factor, BF)
    sent[1], sent[3] = hop(g1, 0, 1), hop(g3, 0, 3)
    g1, keys = in_turn(g1, keys)
    (g2,) = gradient_blocks([blocks[2]], keys, values, rates, factor, BF)
    sent[2] = hop(g2, 0, 2)
    return combined(own, sent)


def gathered(shard):
    parts = [shard] + ring_parts(shard, 1)
    block = call(join_kernel, arr((SIDE, *shard.shape), BF), None, parts, (0, 16 * shard.size))
    return [block] + ring_parts(block, 0)


def shards(queries, key_tokens, value_tokens, learn_rates, fast_init, out_gain):
    tokens, width = key_tokens.shape
    factor = (tokens * lax.axis_size("tok")) ** (-0.5)
    core = lax.axis_index("order")
    tok = lax.axis_index("tok")
    x, y = tok % SIDE, (tok // SIDE) % SIDE
    ring = jnp.arange(SIDE, dtype=jnp.int32)
    r1, r2 = ring[:, None], ring[None, :]
    along_x = (x + jnp.where(core == 0, r1, r2)) % SIDE
    along_y = (y + jnp.where(core == 0, r2, r1)) % SIDE
    place = (along_x * SIDE + along_y).reshape(-1).astype(jnp.int32)
    rates = learn_rates.reshape(1, tokens)
    gain = out_gain.reshape(1, width)

    start, parts = first_totals(place, fast_init, key_tokens, value_tokens, rates, factor)
    shard = start.shape
    size = start.size
    first_step, first_bf = call(
        update_kernel, [arr(shard, F32), arr(shard, BF)], None, (start, *parts), (size, 8 * size)
    )
    blocks = gathered(first_bf)
    parts = second_totals(blocks, key_tokens, value_tokens, rates, factor)
    change, change_bf = call(
        change_kernel,
        [arr(shard, F32), arr(shard, BF)],
        None,
        (start, first_step, *parts),
        (size, 8 * size),
    )
    pairs = [(flat(0, *c), flat(1, *c)) for c in itertools.product(*[range(SIDE)] * 3)]
    earlier = lax.ppermute(change_bf, AXES, pairs)
    closing = call(closing_kernel, arr(shard, BF), None, (start, earlier, change), (size, 8 * size))
    blocks = gathered(closing)
    result = apply_blocks([blocks[0]], queries, None, None)
    result = apply_blocks([blocks[1], blocks[3]], queries, result, None)
    return apply_blocks([blocks[2]], queries, result, gain)


def solution(mesh):
    rows = P(AXES, None)
    return jax.shard_map(
        shards,
        mesh=mesh,
        in_specs=(rows, rows, rows, P(AXES), P(), P()),
        out_specs=rows,
        check_vma=False,
    )
```

```python
import functools
import itertools

import jax
import jax.numpy as jnp
from jax import lax
from jax.experimental import pallas as pl
from jax.experimental.pallas import tpu as pltpu
from jax.sharding import PartitionSpec as P

SIDE = 4
AXES = ("order", "tok")
BF = jnp.bfloat16
F32 = jnp.float32
NT = (((1,), (1,)), ((), ()))
NN = (((1,), (0,)), ((), ()))
VMEM = pl.BlockSpec(memory_space=pltpu.VMEM)
SMEM = pl.BlockSpec(memory_space=pltpu.SMEM)


def flat(core, z, y, x):
    return ((core * SIDE + z % SIDE) * SIDE + y % SIDE) * SIDE + x % SIDE


def hop_pairs(level, step):
    pairs = []
    for core, z, y, x in itertools.product(range(2), *[range(SIDE)] * 3):
        dz = dy = dx = 0
        if level == 2:
            dz = step
        elif (level == 0) == (core == 0):
            dx = step
        else:
            dy = step
        pairs.append((flat(core, z, y, x), flat(core, z + dz, y + dy, x + dx)))
    return pairs


def hop(x, level, step):
    return lax.ppermute(x, AXES, hop_pairs(level, step % SIDE))


HBM = pl.BlockSpec(memory_space=pltpu.HBM)


def call(
    kernel, outs, specs, args, cost, scratch=(), out_spec=VMEM, limit=24 << 20, aliases={}
):
    return pl.pallas_call(
        kernel,
        out_shape=outs,
        in_specs=specs or [VMEM] * len(args),
        out_specs=jax.tree.map(lambda _: out_spec, outs),
        scratch_shapes=scratch,
        input_output_aliases=aliases,
        compiler_params=pltpu.CompilerParams(vmem_limit_bytes=limit),
        cost_estimate=pl.CostEstimate(flops=cost[0], bytes_accessed=cost[1], transcendentals=0),
    )(*args)


def arr(shape, dtype):
    return jax.ShapeDtypeStruct(shape, dtype)


def first_kernel(factor, tile, place, *refs):
    sources, (k_ref, v_ref, rate_ref, b0, b2, own, g1, g3), scratch = refs[:4], refs[4:12], refs[12:]
    w_ref, turned, slab, b1, b3, grads, hiddens, sems = scratch
    copies = [
        pltpu.make_async_copy(src, dst, sems.at[i])
        for i, (src, dst) in enumerate(zip(sources, (w_ref, k_ref, v_ref, rate_ref)))
    ]
    copies[0].start()
    copies[0].wait()
    for copy in copies[1:]:
        copy.start()
    width = w_ref.shape[0]
    lines = width // (SIDE * SIDE)
    for m in range(2):
        part = w_ref[:, m * width : (m + 1) * width].astype(BF)
        turned[m] = part.T.reshape(SIDE * SIDE, lines, width)
    turned[2] = w_ref[:, 2 * width :].astype(BF).reshape(SIDE * SIDE, lines, width)
    for r, block in enumerate((b0, b1, b2, b3)):
        for s in range(SIDE):
            group = place[r * SIDE + s]
            for m in range(3):
                block[s, m] = turned[m, group]
    mine = place[0]
    for m in range(2):
        start = pl.multiple_of(m * width + (mine // SIDE) * 128, 128)
        slab[...] = w_ref[:, pl.ds(start, 128)].T.reshape(SIDE, lines, width)
        own[m] = slab[mine % SIDE]
    own[2] = w_ref[pl.ds(pl.multiple_of(mine * lines, lines), lines), 2 * width :]
    for copy in copies[1:]:
        copy.wait()
    gradient_kernel(factor, tile, 2, b1, b3, k_ref, v_ref, rate_ref, g1, g3, grads, hiddens)


def rows_of(w_refs, m):
    parts = [w[:, m].reshape(-1, w.shape[3]) for w in w_refs]
    return parts[0] if len(parts) == 1 else jnp.concatenate(parts, axis=0)


def gradient_kernel(factor, tile, count, *refs):
    w_refs, (k_ref, v_ref, rate_ref) = refs[:count], refs[count : count + 3]
    outs, (grads, hiddens) = refs[count + 3 : 2 * count + 3], refs[2 * count + 3 :]
    wgu = jnp.concatenate([rows_of(w_refs, 0), rows_of(w_refs, 1)], axis=0)
    wd = rows_of(w_refs, 2)
    units, width = wd.shape
    for i in range(k_ref.shape[0] // tile):
        rows = slice(i * tile, (i + 1) * tile)
        scale = -(rate_ref[:, rows] * factor)
        gu = lax.dot_general(wgu, k_ref[rows, :], NT, preferred_element_type=F32)
        hidden_grad = lax.dot_general(wd, v_ref[rows, :], NT, preferred_element_type=F32) * scale
        gate = gu[:units]
        up = gu[units:]
        sig = 0.5 * jnp.tanh(0.5 * gate) + 0.5
        act = gate * sig
        hiddens[:, rows] = (act * up * scale).astype(BF)
        grads[:units, rows] = (hidden_grad * up * (sig + act * (1.0 - sig))).astype(BF)
        grads[units:, rows] = (hidden_grad * act).astype(BF)
    upper = lax.dot_general(grads[...], k_ref[...], NN, preferred_element_type=F32)
    lower = lax.dot_general(hiddens[...], v_ref[...], NN, preferred_element_type=F32)
    lines = outs[0].shape[2]
    per = units // count
    for b, out in enumerate(outs):
        own = slice(b * per, (b + 1) * per)
        for m, part in enumerate((upper[:units], upper[units:], lower)):
            out[:, m] = part[own].reshape(SIDE, lines, width).astype(out.dtype)


def gradient_blocks(weights, keys, values, rates, factor, dtype, tile=256):
    count = len(weights)
    units = count * weights[0].shape[0] * weights[0].shape[2]
    tokens, width = keys.shape
    return call(
        functools.partial(gradient_kernel, factor, tile, count),
        [arr(w.shape, dtype) for w in weights],
        None,
        (*weights, keys, values, rates),
        (12 * tokens * width * units, 4 * tokens * width),
        [pltpu.VMEM((2 * units, tokens), BF), pltpu.VMEM((units, tokens), BF)],
    )


def near_kernel(own, r1, r3, out):
    out[...] = own[...].astype(F32) + r1[...].astype(F32) + r3[...].astype(F32)


def scatter_kernel(near, r2, keep, s1, s2, s3):
    for s, out in enumerate((keep, s1, s2, s3)):
        out[...] = (near[s] + r2[s].astype(F32)).astype(out.dtype)


def add_kernel(near, r2, out):
    out[...] = (near[...] + r2[...].astype(F32)).astype(out.dtype)


def update_kernel(weights, near, r2, new, new_bf):
    value = weights[...] - (near[...] + r2[...].astype(F32))
    new[...] = value
    new_bf[...] = value.astype(BF)


def change_kernel(start, weights, near, r2, change, change_bf):
    value = (weights[...] - (near[...] + r2[...].astype(F32))) - start[...]
    change[...] = value
    change_bf[...] = value.astype(BF)


def closing_kernel(start, earlier, change, out):
    out[...] = ((start[...] + earlier[...].astype(F32)) + change[...]).astype(BF)


def join_kernel(own, r1, r3, out):
    for s, part in ((0, own), (1, r1), (3, r3)):
        out[s] = part[...]


def join_last_kernel(joined, r2, out):
    del joined
    out[2] = r2[...]


def apply_kernel(tile, count, first, last, *refs):
    refs = list(refs)
    w_refs, q_ref = refs[:count], refs[count]
    refs = refs[count + 1 :]
    gain = refs.pop(0) if last else None
    so_far = None if first else refs.pop(0)
    out = refs.pop(0)
    wgu = jnp.concatenate([rows_of(w_refs, 0), rows_of(w_refs, 1)], axis=0)
    wd = rows_of(w_refs, 2)
    units = wd.shape[0]
    copies = []
    for i in range(q_ref.shape[0] // tile):
        rows = slice(i * tile, (i + 1) * tile)
        gu = lax.dot_general(q_ref[rows, :], wgu, NT, preferred_element_type=F32)
        gate = gu[:, :units]
        up = gu[:, units:]
        act = gate * (0.5 * jnp.tanh(0.5 * gate) + 0.5)
        y = lax.dot_general((act * up).astype(BF), wd, NN, preferred_element_type=F32)
        if so_far is not None:
            y = y + so_far[rows, :]
        if last:
            held, sems = refs
            scale = lax.rsqrt(jnp.mean(y * y, axis=1, keepdims=True) + 1e-06)
            held[rows, :] = (y * scale * gain[...]).astype(BF)
            copies.append(pltpu.make_async_copy(held.at[rows], out.at[rows], sems.at[i]))
            copies[-1].start()
        else:
            out[rows, :] = y
    for copy in copies:
        copy.wait()


def apply_blocks(weights, queries, so_far, gain, tile=256):
    count = len(weights)
    units = count * weights[0].shape[0] * weights[0].shape[2]
    tokens, width = queries.shape
    first, last = so_far is None, gain is not None
    args = (*weights, queries) + ((gain,) if last else ()) + (() if first else (so_far,))
    scratch = ()
    if last:
        scratch = [pltpu.VMEM((tokens, width), BF), pltpu.SemaphoreType.DMA((tokens // tile,))]
    return call(
        functools.partial(apply_kernel, tile, count, first, last),
        arr((tokens, width), BF if last else F32),
        None,
        args,
        (6 * tokens * width * units, 6 * tokens * width),
        scratch,
        out_spec=HBM if last else VMEM,
    )


def near_sum(own, r1, r3):
    size = own.size
    return call(near_kernel, arr(own.shape, F32), None, (own, r1, r3), (2 * size, 12 * size))


def in_turn(first, *later):
    return lax.optimization_barrier((first, *later))


def combined(own, sent):
    shard = own.shape[1:]
    size = own.size
    keep, *out = call(
        scatter_kernel,
        [arr(shard, F32)] + [arr(shard, BF)] * 3,
        None,
        (near_sum(own, sent[1], sent[3]), sent[2]),
        (size, 8 * size),
    )
    got = {r: hop(out[r - 1], 1, r) for r in (1, 3, 2)}
    near = near_sum(keep, got[1], got[3])
    part = call(add_kernel, arr(shard, BF), None, (near, got[2]), (size, 3 * size))
    got = {r: hop(part, 2, r) for r in (1, 3, 2)}
    return near_sum(part, got[1], got[3]), got[2]


def first_totals(place, weights, keys, values, rates, factor, tile=256):
    sources = (weights, keys, values, rates)
    tokens, width = keys.shape
    lines = width // (SIDE * SIDE)
    block = (SIDE, 3, lines, width)
    units = 2 * SIDE * lines
    keys, values, rates, b0, b2, start, g1, g3 = call(
        functools.partial(first_kernel, factor, tile),
        [arr(keys.shape, BF), arr(values.shape, BF), arr(rates.shape, F32)]
        + [arr(block, BF)] * 2
        + [arr(block[1:], F32)]
        + [arr(block, BF)] * 2,
        [SMEM] + [HBM] * 4,
        (place, *(pltpu.with_memory_space_constraint(x, pltpu.HBM) for x in sources)),
        (12 * tokens * width * units, 4 * tokens * width),
        [
            pltpu.VMEM(weights.shape, F32),
            pltpu.VMEM((3, SIDE * SIDE, lines, width), BF),
            pltpu.VMEM((SIDE, lines, width), F32),
            pltpu.VMEM(block, BF),
            pltpu.VMEM(block, BF),
            pltpu.VMEM((2 * units, tokens), BF),
            pltpu.VMEM((units, tokens), BF),
            pltpu.SemaphoreType.DMA((4,)),
        ],
        limit=32 << 20,
    )
    sent = {1: hop(g1, 0, 1), 3: hop(g3, 0, 3)}
    (g2,) = gradient_blocks([b2], keys, values, rates, factor, BF)
    sent[2] = hop(g2, 0, 2)
    (own,) = gradient_blocks([b0], keys, values, rates, factor, F32)
    return start, (keys, values, rates), combined(own, sent)


def gathered(shard):
    got = {r: hop(shard, 1, -r) for r in (1, 3, 2)}
    block = arr((SIDE, *shard.shape), BF)
    size = shard.size
    joined = call(join_kernel, block, None, (shard, got[1], got[3]), (0, 12 * size))
    return call(
        join_last_kernel, block, None, (joined, got[2]), (0, 4 * size), aliases={0: 0}
    )


def second_totals(shard, keys, values, rates, factor):
    block = gathered(shard)
    b1, b3 = hop(block, 0, -1), hop(block, 0, -3)
    (own,) = gradient_blocks([block], keys, values, rates, factor, F32)
    own, keys, block = in_turn(own, keys, block)
    b2 = hop(block, 0, -2)
    sent = {}
    g1, g3 = gradient_blocks([b1, b3], keys, values, rates, factor, BF)
    sent[1], sent[3] = hop(g1, 0, 1), hop(g3, 0, 3)
    g1, keys = in_turn(g1, keys)
    (g2,) = gradient_blocks([b2], keys, values, rates, factor, BF)
    sent[2] = hop(g2, 0, 2)
    return combined(own, sent)


def applied(shard, queries, gain):
    block = gathered(shard)
    b1, b3 = hop(block, 0, -1), hop(block, 0, -3)
    result = apply_blocks([block], queries, None, None)
    result, block = in_turn(result, block)
    b2 = hop(block, 0, -2)
    result = apply_blocks([b1, b3], queries, result, None)
    return apply_blocks([b2], queries, result, gain)


def shards(queries, key_tokens, value_tokens, learn_rates, fast_init, out_gain):
    tokens, width = key_tokens.shape
    factor = (tokens * lax.axis_size("tok")) ** (-0.5)
    core = lax.axis_index("order")
    tok = lax.axis_index("tok")
    x, y = tok % SIDE, (tok // SIDE) % SIDE
    ring = jnp.arange(SIDE, dtype=jnp.int32)
    r1, r2 = ring[:, None], ring[None, :]
    along_x = (x + jnp.where(core == 0, r1, r2)) % SIDE
    along_y = (y + jnp.where(core == 0, r2, r1)) % SIDE
    place = (along_x * SIDE + along_y).reshape(-1).astype(jnp.int32)
    rates = learn_rates.reshape(1, tokens)
    gain = out_gain.reshape(1, width)

    start, tokens_in, parts = first_totals(place, fast_init, key_tokens, value_tokens, rates, factor)
    shard = start.shape
    size = start.size
    first_step, shard_bf = call(
        update_kernel, [arr(shard, F32), arr(shard, BF)], None, (start, *parts), (size, 8 * size)
    )
    parts = second_totals(shard_bf, *tokens_in, factor)
    change, change_bf = call(
        change_kernel,
        [arr(shard, F32), arr(shard, BF)],
        None,
        (start, first_step, *parts),
        (size, 8 * size),
    )
    pairs = [(flat(0, *c), flat(1, *c)) for c in itertools.product(*[range(SIDE)] * 3)]
    earlier = lax.ppermute(change_bf, AXES, pairs)
    closing = call(closing_kernel, arr(shard, BF), None, (start, earlier, change), (size, 8 * size))
    return applied(closing, queries, gain)


def solution(mesh):
    rows = P(AXES, None)
    return jax.shard_map(
        shards,
        mesh=mesh,
        in_specs=(rows, rows, rows, P(AXES), P(), P()),
        out_specs=rows,
        check_vma=False,
    )
```

```python
import functools
import itertools

import jax
import jax.numpy as jnp
from jax import lax
from jax.experimental import pallas as pl
from jax.experimental.pallas import tpu as pltpu
from jax.sharding import PartitionSpec as P

SIDE = 4
AXES = ("order", "tok")
BF = jnp.bfloat16
F32 = jnp.float32
NT = (((1,), (1,)), ((), ()))
NN = (((1,), (0,)), ((), ()))
VMEM = pl.BlockSpec(memory_space=pltpu.VMEM)
SMEM = pl.BlockSpec(memory_space=pltpu.SMEM)


def flat(core, z, y, x):
    return ((core * SIDE + z % SIDE) * SIDE + y % SIDE) * SIDE + x % SIDE


def hop_pairs(level, step):
    pairs = []
    for core, z, y, x in itertools.product(range(2), *[range(SIDE)] * 3):
        dz = dy = dx = 0
        if level == 2:
            dz = step
        elif (level == 0) == (core == 0):
            dx = step
        else:
            dy = step
        pairs.append((flat(core, z, y, x), flat(core, z + dz, y + dy, x + dx)))
    return pairs


def hop(x, level, step):
    return lax.ppermute(x, AXES, hop_pairs(level, step % SIDE))


HBM = pl.BlockSpec(memory_space=pltpu.HBM)


def call(
    kernel, outs, specs, args, cost, scratch=(), out_spec=VMEM, limit=24 << 20, aliases={}
):
    return pl.pallas_call(
        kernel,
        out_shape=outs,
        in_specs=specs or [VMEM] * len(args),
        out_specs=jax.tree.map(lambda _: out_spec, outs),
        scratch_shapes=scratch,
        input_output_aliases=aliases,
        compiler_params=pltpu.CompilerParams(vmem_limit_bytes=limit),
        cost_estimate=pl.CostEstimate(flops=cost[0], bytes_accessed=cost[1], transcendentals=0),
    )(*args)


def arr(shape, dtype):
    return jax.ShapeDtypeStruct(shape, dtype)


def first_kernel(factor, tile, place, *refs):
    sources, outs, scratch = refs[:4], refs[4:12], refs[12:]
    k_ref, v_ref, rate_ref, b0, b1, b3, own, g2 = outs
    w_ref, turned, slab, b2, grads, hiddens, sems = scratch
    copies = []
    for src, dst in zip(sources, (w_ref, k_ref, v_ref, rate_ref)):
        count = sems.shape[1] if src.shape[0] > 1 else 1
        rows = src.shape[0] // count
        for j in range(count):
            part = pl.ds(j * rows, rows)
            sem = sems.at[len(copies) // sems.shape[1], j]
            copies.append(pltpu.make_async_copy(src.at[part], dst.at[part], sem))
            copies[-1].start()
    for copy in copies[: sems.shape[1]]:
        copy.wait()
    width = w_ref.shape[0]
    lines = width // (SIDE * SIDE)
    for m in range(2):
        part = w_ref[:, m * width : (m + 1) * width].astype(BF)
        turned[m] = part.T.reshape(SIDE * SIDE, lines, width)
    turned[2] = w_ref[:, 2 * width :].astype(BF).reshape(SIDE * SIDE, lines, width)
    for r, block in enumerate((b0, b1, b2, b3)):
        for s in range(SIDE):
            group = place[r * SIDE + s]
            for m in range(3):
                block[s, m] = turned[m, group]
    mine = place[0]
    for m in range(2):
        start = pl.multiple_of(m * width + (mine // SIDE) * 128, 128)
        slab[...] = w_ref[:, pl.ds(start, 128)].T.reshape(SIDE, lines, width)
        own[m] = slab[mine % SIDE]
    own[2] = w_ref[pl.ds(pl.multiple_of(mine * lines, lines), lines), 2 * width :]
    for copy in copies[sems.shape[1] :]:
        copy.wait()
    gradient_kernel(factor, tile, 1, b2, k_ref, v_ref, rate_ref, g2, grads, hiddens)


def rows_of(w_refs, m):
    parts = [w[:, m].reshape(-1, w.shape[3]) for w in w_refs]
    return parts[0] if len(parts) == 1 else jnp.concatenate(parts, axis=0)


def gradient_kernel(factor, tile, count, *refs):
    w_refs, (k_ref, v_ref, rate_ref) = refs[:count], refs[count : count + 3]
    outs, (grads, hiddens) = refs[count + 3 : 2 * count + 3], refs[2 * count + 3 :]
    wgu = jnp.concatenate([rows_of(w_refs, 0), rows_of(w_refs, 1)], axis=0)
    wd = rows_of(w_refs, 2)
    units, width = wd.shape
    for i in range(k_ref.shape[0] // tile):
        rows = slice(i * tile, (i + 1) * tile)
        scale = -(rate_ref[:, rows] * factor)
        gu = lax.dot_general(wgu, k_ref[rows, :], NT, preferred_element_type=F32)
        hidden_grad = lax.dot_general(wd, v_ref[rows, :], NT, preferred_element_type=F32) * scale
        gate = gu[:units]
        up = gu[units:]
        sig = 0.5 * jnp.tanh(0.5 * gate) + 0.5
        act = gate * sig
        hiddens[:, rows] = (act * up * scale).astype(BF)
        grads[:units, rows] = (hidden_grad * up * (sig + act * (1.0 - sig))).astype(BF)
        grads[units:, rows] = (hidden_grad * act).astype(BF)
    upper = lax.dot_general(grads[...], k_ref[...], NN, preferred_element_type=F32)
    lower = lax.dot_general(hiddens[...], v_ref[...], NN, preferred_element_type=F32)
    lines = outs[0].shape[2]
    per = units // count
    for b, out in enumerate(outs):
        own = slice(b * per, (b + 1) * per)
        for m, part in enumerate((upper[:units], upper[units:], lower)):
            out[:, m] = part[own].reshape(SIDE, lines, width).astype(out.dtype)


def gradient_blocks(weights, keys, values, rates, factor, dtype, tile=256):
    count = len(weights)
    units = count * weights[0].shape[0] * weights[0].shape[2]
    tokens, width = keys.shape
    return call(
        functools.partial(gradient_kernel, factor, tile, count),
        [arr(w.shape, dtype) for w in weights],
        None,
        (*weights, keys, values, rates),
        (12 * tokens * width * units, 4 * tokens * width),
        [pltpu.VMEM((2 * units, tokens), BF), pltpu.VMEM((units, tokens), BF)],
    )


def far_kernel(own, r2, out):
    out[...] = own[...] + r2[...].astype(F32)


def scatter_kernel(far, r1, r3, keep, s1, s2, s3):
    for s, out in enumerate((keep, s1, s2, s3)):
        out[...] = (far[s] + r1[s].astype(F32) + r3[s].astype(F32)).astype(out.dtype)


def grow_kernel(own, part, out):
    out[...] = own[...].astype(F32) + part[...].astype(F32)


def add_kernel(own, part, out):
    out[...] = (own[...] + part[...].astype(F32)).astype(out.dtype)


def update_kernel(weights, own, part, new, new_bf):
    value = weights[...] - (own[...] + part[...].astype(F32))
    new[...] = value
    new_bf[...] = value.astype(BF)


def change_kernel(start, weights, own, part, change, change_bf):
    value = (weights[...] - (own[...] + part[...].astype(F32))) - start[...]
    change[...] = value
    change_bf[...] = value.astype(BF)


def closing_kernel(start, earlier, change, out):
    out[...] = ((start[...] + earlier[...].astype(F32)) + change[...]).astype(BF)


def join_kernel(slot, joined, part, out):
    del joined
    out[slot] = part[...]


def join_first_kernel(own, part, out):
    out[0] = own[...]
    out[1] = part[...]


def apply_kernel(tile, count, first, last, *refs):
    refs = list(refs)
    w_refs, q_ref = refs[:count], refs[count]
    refs = refs[count + 1 :]
    gain = refs.pop(0) if last else None
    so_far = None if first else refs.pop(0)
    out = refs.pop(0)
    wgu = jnp.concatenate([rows_of(w_refs, 0), rows_of(w_refs, 1)], axis=0)
    wd = rows_of(w_refs, 2)
    units = wd.shape[0]
    copies = []
    for i in range(q_ref.shape[0] // tile):
        rows = slice(i * tile, (i + 1) * tile)
        gu = lax.dot_general(q_ref[rows, :], wgu, NT, preferred_element_type=F32)
        gate = gu[:, :units]
        up = gu[:, units:]
        act = gate * (0.5 * jnp.tanh(0.5 * gate) + 0.5)
        y = lax.dot_general((act * up).astype(BF), wd, NN, preferred_element_type=F32)
        if so_far is not None:
            y = y + so_far[rows, :]
        if last:
            held, sems = refs
            scale = lax.rsqrt(jnp.mean(y * y, axis=1, keepdims=True) + 1e-06)
            held[rows, :] = (y * scale * gain[...]).astype(BF)
            copies.append(pltpu.make_async_copy(held.at[rows], out.at[rows], sems.at[i]))
            copies[-1].start()
        else:
            out[rows, :] = y
    for copy in copies:
        copy.wait()


def apply_blocks(weights, queries, so_far, gain, tile=256):
    count = len(weights)
    units = count * weights[0].shape[0] * weights[0].shape[2]
    tokens, width = queries.shape
    first, last = so_far is None, gain is not None
    args = (*weights, queries) + ((gain,) if last else ()) + (() if first else (so_far,))
    scratch = ()
    if last:
        scratch = [pltpu.VMEM((tokens, width), BF), pltpu.SemaphoreType.DMA((tokens // tile,))]
    return call(
        functools.partial(apply_kernel, tile, count, first, last),
        arr((tokens, width), BF if last else F32),
        None,
        args,
        (6 * tokens * width * units, 6 * tokens * width),
        scratch,
        out_spec=HBM if last else VMEM,
    )


def in_turn(first, *later):
    return lax.optimization_barrier((first, *later))


def ring_parts(x, level):
    return [hop(x, level, -r) for r in range(1, SIDE)]


def grown(total, parts):
    size = total.size
    for part in parts:
        total = call(grow_kernel, arr(total.shape, F32), None, (total, part), (size, 8 * size))
    return total


def combined(own, sent):
    shard = own.shape[1:]
    size = own.size
    far = call(far_kernel, arr(own.shape, F32), None, (own, sent[2]), (size, 10 * size))
    keep, *out = call(
        scatter_kernel,
        [arr(shard, F32)] + [arr(shard, BF)] * 3,
        None,
        (far, sent[1], sent[3]),
        (2 * size, 10 * size),
    )
    got = [hop(x, 1, r + 1) for r, x in enumerate(out)]
    part = call(add_kernel, arr(shard, BF), None, (grown(keep, got[:2]), got[2]), (size, 3 * size))
    got = ring_parts(part, 2)
    return grown(part, got[:2]), got[2]


def first_totals(place, weights, keys, values, rates, factor, tile=256):
    sources = (weights, keys, values, rates)
    tokens, width = keys.shape
    lines = width // (SIDE * SIDE)
    block = (SIDE, 3, lines, width)
    units = SIDE * lines
    keys, values, rates, b0, b1, b3, start, g2 = call(
        functools.partial(first_kernel, factor, tile),
        [arr(keys.shape, BF), arr(values.shape, BF), arr(rates.shape, F32)]
        + [arr(block, BF)] * 3
        + [arr(block[1:], F32), arr(block, BF)],
        [SMEM] + [HBM] * 4,
        (place, *(pltpu.with_memory_space_constraint(x, pltpu.HBM) for x in sources)),
        (12 * tokens * width * units, 4 * tokens * width),
        [
            pltpu.VMEM(weights.shape, F32),
            pltpu.VMEM((3, SIDE * SIDE, lines, width), BF),
            pltpu.VMEM((SIDE, lines, width), F32),
            pltpu.VMEM(block, BF),
            pltpu.VMEM((2 * units, tokens), BF),
            pltpu.VMEM((units, tokens), BF),
            pltpu.SemaphoreType.DMA((4, 4)),
        ],
        limit=32 << 20,
    )
    sent = {2: hop(g2, 0, 2)}
    g1, g3 = gradient_blocks([b1, b3], keys, values, rates, factor, BF)
    sent[1], sent[3] = hop(g1, 0, 1), hop(g3, 0, 3)
    (own,) = gradient_blocks([b0], keys, values, rates, factor, F32)
    return start, (keys, values, rates), combined(own, sent)


def gathered(shard):
    parts = ring_parts(shard, 1)
    block = arr((SIDE, *shard.shape), BF)
    cost = (0, 4 * shard.size)
    joined = call(join_first_kernel, block, None, (shard, parts[0]), cost)
    for r in (2, 3):
        kernel = functools.partial(join_kernel, r)
        joined = call(kernel, block, None, (joined, parts[r - 1]), cost, aliases={0: 0})
    return joined


def second_totals(shard, keys, values, rates, factor):
    block = gathered(shard)
    b2, b1, b3 = hop(block, 0, -2), hop(block, 0, -1), hop(block, 0, -3)
    (own,) = gradient_blocks([block], keys, values, rates, factor, F32)
    own, keys = in_turn(own, keys)
    (g2,) = gradient_blocks([b2], keys, values, rates, factor, BF)
    sent = {2: hop(g2, 0, 2)}
    g2, keys = in_turn(g2, keys)
    g1, g3 = gradient_blocks([b1, b3], keys, values, rates, factor, BF)
    sent[1], sent[3] = hop(g1, 0, 1), hop(g3, 0, 3)
    return combined(own, sent)


def applied(shard, queries, gain):
    block = gathered(shard)
    b2, b1, b3 = hop(block, 0, -2), hop(block, 0, -1), hop(block, 0, -3)
    result = apply_blocks([block], queries, None, None)
    result = apply_blocks([b2], queries, result, None)
    return apply_blocks([b1, b3], queries, result, gain)


def shards(queries, key_tokens, value_tokens, learn_rates, fast_init, out_gain):
    tokens, width = key_tokens.shape
    factor = (tokens * lax.axis_size("tok")) ** (-0.5)
    core = lax.axis_index("order")
    tok = lax.axis_index("tok")
    x, y = tok % SIDE, (tok // SIDE) % SIDE
    ring = jnp.arange(SIDE, dtype=jnp.int32)
    r1, r2 = ring[:, None], ring[None, :]
    along_x = (x + jnp.where(core == 0, r1, r2)) % SIDE
    along_y = (y + jnp.where(core == 0, r2, r1)) % SIDE
    place = (along_x * SIDE + along_y).reshape(-1).astype(jnp.int32)
    rates = learn_rates.reshape(1, tokens)
    gain = out_gain.reshape(1, width)

    start, tokens_in, parts = first_totals(place, fast_init, key_tokens, value_tokens, rates, factor)
    shard = start.shape
    size = start.size
    first_step, shard_bf = call(
        update_kernel, [arr(shard, F32), arr(shard, BF)], None, (start, *parts), (size, 8 * size)
    )
    parts = second_totals(shard_bf, *tokens_in, factor)
    change, change_bf = call(
        change_kernel,
        [arr(shard, F32), arr(shard, BF)],
        None,
        (start, first_step, *parts),
        (size, 8 * size),
    )
    pairs = [(flat(0, *c), flat(1, *c)) for c in itertools.product(*[range(SIDE)] * 3)]
    earlier = lax.ppermute(change_bf, AXES, pairs)
    closing = call(closing_kernel, arr(shard, BF), None, (start, earlier, change), (size, 8 * size))
    return applied(closing, queries, gain)


def solution(mesh):
    rows = P(AXES, None)
    return jax.shard_map(
        shards,
        mesh=mesh,
        in_specs=(rows, rows, rows, P(AXES), P(), P()),
        out_specs=rows,
        check_vma=False,
    )
```

```python
import functools
import itertools

import jax
import jax.numpy as jnp
from jax import lax
from jax.experimental import pallas as pl
from jax.experimental.pallas import tpu as pltpu
from jax.sharding import PartitionSpec as P

SIDE = 4
AXES = ("order", "tok")
BF = jnp.bfloat16
F32 = jnp.float32
NT = (((1,), (1,)), ((), ()))
NN = (((1,), (0,)), ((), ()))
VMEM = pl.BlockSpec(memory_space=pltpu.VMEM)
SMEM = pl.BlockSpec(memory_space=pltpu.SMEM)


def flat(core, z, y, x):
    return ((core * SIDE + z % SIDE) * SIDE + y % SIDE) * SIDE + x % SIDE


def hop_pairs(level, step):
    pairs = []
    for core, z, y, x in itertools.product(range(2), *[range(SIDE)] * 3):
        dz = dy = dx = 0
        if level == 2:
            dz = step
        elif (level == 0) == (core == 0):
            dx = step
        else:
            dy = step
        pairs.append((flat(core, z, y, x), flat(core, z + dz, y + dy, x + dx)))
    return pairs


def hop(x, level, step):
    return lax.ppermute(x, AXES, hop_pairs(level, step % SIDE))


HBM = pl.BlockSpec(memory_space=pltpu.HBM)


def call(
    kernel, outs, specs, args, cost, scratch=(), out_spec=VMEM, limit=24 << 20, aliases={}
):
    return pl.pallas_call(
        kernel,
        out_shape=outs,
        in_specs=specs or [VMEM] * len(args),
        out_specs=jax.tree.map(lambda _: out_spec, outs),
        scratch_shapes=scratch,
        input_output_aliases=aliases,
        compiler_params=pltpu.CompilerParams(vmem_limit_bytes=limit),
        cost_estimate=pl.CostEstimate(flops=cost[0], bytes_accessed=cost[1], transcendentals=0),
    )(*args)


def arr(shape, dtype):
    return jax.ShapeDtypeStruct(shape, dtype)


def first_kernel(factor, tile, place, *refs):
    sources, outs, scratch = refs[:4], refs[4:12], refs[12:]
    k_ref, v_ref, rate_ref, b0, b1, b3, own, g2 = outs
    w_ref, turned, slab, b2, grads, hiddens, sems = scratch
    copies = []
    for src, dst in zip(sources, (w_ref, k_ref, v_ref, rate_ref)):
        count = sems.shape[1] if src.shape[0] > 1 else 1
        rows = src.shape[0] // count
        for j in range(count):
            part = pl.ds(j * rows, rows)
            sem = sems.at[len(copies) // sems.shape[1], j]
            copies.append(pltpu.make_async_copy(src.at[part], dst.at[part], sem))
            copies[-1].start()
    for copy in copies[: sems.shape[1]]:
        copy.wait()
    width = w_ref.shape[0]
    lines = width // (SIDE * SIDE)
    for m in range(2):
        part = w_ref[:, m * width : (m + 1) * width].astype(BF)
        turned[m] = part.T.reshape(SIDE * SIDE, lines, width)
    turned[2] = w_ref[:, 2 * width :].astype(BF).reshape(SIDE * SIDE, lines, width)
    for r, block in enumerate((b0, b1, b2, b3)):
        for s in range(SIDE):
            group = place[r * SIDE + s]
            for m in range(3):
                block[s, m] = turned[m, group]
    mine = place[0]
    for m in range(2):
        start = pl.multiple_of(m * width + (mine // SIDE) * 128, 128)
        slab[...] = w_ref[:, pl.ds(start, 128)].T.reshape(SIDE, lines, width)
        own[m] = slab[mine % SIDE]
    own[2] = w_ref[pl.ds(pl.multiple_of(mine * lines, lines), lines), 2 * width :]
    for copy in copies[sems.shape[1] :]:
        copy.wait()
    gradient_kernel(factor, tile, 1, b2, k_ref, v_ref, rate_ref, g2, grads, hiddens)


def rows_of(w_refs, m):
    parts = [w[:, m].reshape(-1, w.shape[3]) for w in w_refs]
    return parts[0] if len(parts) == 1 else jnp.concatenate(parts, axis=0)


def gradient_kernel(factor, tile, count, *refs):
    w_refs, (k_ref, v_ref, rate_ref) = refs[:count], refs[count : count + 3]
    outs, (grads, hiddens) = refs[count + 3 : 2 * count + 3], refs[2 * count + 3 :]
    wgu = jnp.concatenate([rows_of(w_refs, 0), rows_of(w_refs, 1)], axis=0)
    wd = rows_of(w_refs, 2)
    units, width = wd.shape
    for i in range(k_ref.shape[0] // tile):
        rows = slice(i * tile, (i + 1) * tile)
        scale = -(rate_ref[:, rows] * factor)
        gu = lax.dot_general(wgu, k_ref[rows, :], NT, preferred_element_type=F32)
        hidden_grad = lax.dot_general(wd, v_ref[rows, :], NT, preferred_element_type=F32) * scale
        gate = gu[:units]
        up = gu[units:]
        sig = 0.5 * jnp.tanh(0.5 * gate) + 0.5
        act = gate * sig
        hiddens[:, rows] = (act * up * scale).astype(BF)
        grads[:units, rows] = (hidden_grad * up * (sig + act * (1.0 - sig))).astype(BF)
        grads[units:, rows] = (hidden_grad * act).astype(BF)
    upper = lax.dot_general(grads[...], k_ref[...], NN, preferred_element_type=F32)
    lower = lax.dot_general(hiddens[...], v_ref[...], NN, preferred_element_type=F32)
    lines = outs[0].shape[2]
    per = units // count
    for b, out in enumerate(outs):
        own = slice(b * per, (b + 1) * per)
        for m, part in enumerate((upper[:units], upper[units:], lower)):
            out[:, m] = part[own].reshape(SIDE, lines, width).astype(out.dtype)


def gradient_blocks(weights, keys, values, rates, factor, dtype, tile=256):
    count = len(weights)
    units = count * weights[0].shape[0] * weights[0].shape[2]
    tokens, width = keys.shape
    return call(
        functools.partial(gradient_kernel, factor, tile, count),
        [arr(w.shape, dtype) for w in weights],
        None,
        (*weights, keys, values, rates),
        (12 * tokens * width * units, 4 * tokens * width),
        [pltpu.VMEM((2 * units, tokens), BF), pltpu.VMEM((units, tokens), BF)],
    )


def far_kernel(own, r2, out):
    out[...] = own[...] + r2[...].astype(F32)


def scatter_kernel(far, r1, r3, keep, s1, s2, s3):
    for s, out in enumerate((keep, s1, s2, s3)):
        out[...] = (far[s] + r1[s].astype(F32) + r3[s].astype(F32)).astype(out.dtype)


def total_of(own, r1, r2, r3):
    return (own[...].astype(F32) + r1[...].astype(F32)) + (r2[...].astype(F32) + r3[...].astype(F32))


def add_kernel(own, r1, r2, r3, out):
    out[...] = total_of(own, r1, r2, r3).astype(out.dtype)


def update_kernel(weights, own, r1, r2, r3, new, new_bf):
    value = weights[...] - total_of(own, r1, r2, r3)
    new[...] = value
    new_bf[...] = value.astype(BF)


def change_kernel(start, weights, own, r1, r2, r3, change, change_bf):
    value = (weights[...] - total_of(own, r1, r2, r3)) - start[...]
    change[...] = value
    change_bf[...] = value.astype(BF)


def closing_kernel(start, earlier, change, out):
    out[...] = ((start[...] + earlier[...].astype(F32)) + change[...]).astype(BF)


def join_all_kernel(own, r1, r2, r3, out):
    for s, part in enumerate((own, r1, r2, r3)):
        out[s] = part[...]


def join_first_kernel(own, part, out, token):
    out[0] = own[...]
    out[1] = part[...]
    token[...] = own[0, : token.shape[0], : token.shape[1]]


def join_kernel(slot, joined, part, *rest):
    rest[-1][slot] = part[...]


def apply_kernel(tile, count, first, last, *refs):
    refs = list(refs)
    w_refs, q_ref = refs[:count], refs[count]
    refs = refs[count + 1 :]
    gain = refs.pop(0) if last else None
    so_far = None if first else refs.pop(0)
    out = refs.pop(0)
    wgu = jnp.concatenate([rows_of(w_refs, 0), rows_of(w_refs, 1)], axis=0)
    wd = rows_of(w_refs, 2)
    units = wd.shape[0]
    copies = []
    for i in range(q_ref.shape[0] // tile):
        rows = slice(i * tile, (i + 1) * tile)
        gu = lax.dot_general(q_ref[rows, :], wgu, NT, preferred_element_type=F32)
        gate = gu[:, :units]
        up = gu[:, units:]
        act = gate * (0.5 * jnp.tanh(0.5 * gate) + 0.5)
        y = lax.dot_general((act * up).astype(BF), wd, NN, preferred_element_type=F32)
        if so_far is not None:
            y = y + so_far[rows, :]
        if last:
            held, sems = refs
            scale = lax.rsqrt(jnp.mean(y * y, axis=1, keepdims=True) + 1e-06)
            held[rows, :] = (y * scale * gain[...]).astype(BF)
            copies.append(pltpu.make_async_copy(held.at[rows], out.at[rows], sems.at[i]))
            copies[-1].start()
        else:
            out[rows, :] = y
    for copy in copies:
        copy.wait()


def apply_blocks(weights, queries, so_far, gain, tile=256):
    count = len(weights)
    units = count * weights[0].shape[0] * weights[0].shape[2]
    tokens, width = queries.shape
    first, last = so_far is None, gain is not None
    args = (*weights, queries) + ((gain,) if last else ()) + (() if first else (so_far,))
    scratch = ()
    if last:
        scratch = [pltpu.VMEM((tokens, width), BF), pltpu.SemaphoreType.DMA((tokens // tile,))]
    return call(
        functools.partial(apply_kernel, tile, count, first, last),
        arr((tokens, width), BF if last else F32),
        None,
        args,
        (6 * tokens * width * units, 6 * tokens * width),
        scratch,
        out_spec=HBM if last else VMEM,
    )


def in_turn(first, *later):
    return lax.optimization_barrier((first, *later))


def ring_parts(x, level):
    return [hop(x, level, -r) for r in range(1, SIDE)]


def combined(own, sent):
    shard = own.shape[1:]
    size = own.size
    far = call(far_kernel, arr(own.shape, F32), None, (own, sent[2]), (size, 10 * size))
    keep, *out = call(
        scatter_kernel,
        [arr(shard, F32)] + [arr(shard, BF)] * 3,
        None,
        (far, sent[1], sent[3]),
        (2 * size, 10 * size),
    )
    got = [hop(x, 1, r + 1) for r, x in enumerate(out)]
    part = call(add_kernel, arr(shard, BF), None, (keep, *got), (size, 3 * size))
    return [part] + ring_parts(part, 2)


def first_totals(place, weights, keys, values, rates, factor, tile=256):
    sources = (weights, keys, values, rates)
    tokens, width = keys.shape
    lines = width // (SIDE * SIDE)
    block = (SIDE, 3, lines, width)
    units = SIDE * lines
    keys, values, rates, b0, b1, b3, start, g2 = call(
        functools.partial(first_kernel, factor, tile),
        [arr(keys.shape, BF), arr(values.shape, BF), arr(rates.shape, F32)]
        + [arr(block, BF)] * 3
        + [arr(block[1:], F32), arr(block, BF)],
        [SMEM] + [HBM] * 4,
        (place, *(pltpu.with_memory_space_constraint(x, pltpu.HBM) for x in sources)),
        (12 * tokens * width * units, 4 * tokens * width),
        [
            pltpu.VMEM(weights.shape, F32),
            pltpu.VMEM((3, SIDE * SIDE, lines, width), BF),
            pltpu.VMEM((SIDE, lines, width), F32),
            pltpu.VMEM(block, BF),
            pltpu.VMEM((2 * units, tokens), BF),
            pltpu.VMEM((units, tokens), BF),
            pltpu.SemaphoreType.DMA((4, 4)),
        ],
        limit=32 << 20,
    )
    sent = {2: hop(g2, 0, 2)}
    g1, g3 = gradient_blocks([b1, b3], keys, values, rates, factor, BF)
    sent[1], sent[3] = hop(g1, 0, 1), hop(g3, 0, 3)
    (own,) = gradient_blocks([b0], keys, values, rates, factor, F32)
    return start, (keys, values, rates), combined(own, sent)


def order_pairs():
    return [(flat(0, *c), flat(1, *c)) for c in itertools.product(*[range(SIDE)] * 3)]


def gathered(shard, in_step):
    parts = ring_parts(shard, 1)
    block = arr((SIDE, *shard.shape), BF)
    cost = (0, 4 * shard.size)
    if not in_step:
        return call(join_all_kernel, block, None, (shard, *parts), cost)
    outs = [block, arr((16, 128), BF)]
    joined, token = call(join_first_kernel, outs, None, (shard, parts[0]), cost)
    more = [[], [lax.ppermute(token, AXES, order_pairs())]]
    for r in (2, 3):
        kernel = functools.partial(join_kernel, r)
        args = (joined, parts[r - 1], *more[r - 2])
        joined = call(kernel, block, None, args, cost, aliases={0: 0})
    return joined


def second_totals(shard, keys, values, rates, factor):
    block = gathered(shard, True)
    b2, b1, b3 = hop(block, 0, -2), hop(block, 0, -1), hop(block, 0, -3)
    (own,) = gradient_blocks([block], keys, values, rates, factor, F32)
    own, keys = in_turn(own, keys)
    (g2,) = gradient_blocks([b2], keys, values, rates, factor, BF)
    sent = {2: hop(g2, 0, 2)}
    g2, keys = in_turn(g2, keys)
    g1, g3 = gradient_blocks([b1, b3], keys, values, rates, factor, BF)
    sent[1], sent[3] = hop(g1, 0, 1), hop(g3, 0, 3)
    return combined(own, sent)


def applied(shard, queries, gain):
    block = gathered(shard, False)
    b2, b1, b3 = hop(block, 0, -2), hop(block, 0, -1), hop(block, 0, -3)
    result = apply_blocks([block], queries, None, None)
    result = apply_blocks([b2], queries, result, None)
    return apply_blocks([b1, b3], queries, result, gain)


def shards(queries, key_tokens, value_tokens, learn_rates, fast_init, out_gain):
    tokens, width = key_tokens.shape
    factor = (tokens * lax.axis_size("tok")) ** (-0.5)
    core = lax.axis_index("order")
    tok = lax.axis_index("tok")
    x, y = tok % SIDE, (tok // SIDE) % SIDE
    ring = jnp.arange(SIDE, dtype=jnp.int32)
    r1, r2 = ring[:, None], ring[None, :]
    along_x = (x + jnp.where(core == 0, r1, r2)) % SIDE
    along_y = (y + jnp.where(core == 0, r2, r1)) % SIDE
    place = (along_x * SIDE + along_y).reshape(-1).astype(jnp.int32)
    rates = learn_rates.reshape(1, tokens)
    gain = out_gain.reshape(1, width)

    start, tokens_in, parts = first_totals(place, fast_init, key_tokens, value_tokens, rates, factor)
    shard = start.shape
    size = start.size
    first_step, shard_bf = call(
        update_kernel, [arr(shard, F32), arr(shard, BF)], None, (start, *parts), (size, 8 * size)
    )
    parts = second_totals(shard_bf, *tokens_in, factor)
    change, change_bf = call(
        change_kernel,
        [arr(shard, F32), arr(shard, BF)],
        None,
        (start, first_step, *parts),
        (size, 8 * size),
    )
    earlier = lax.ppermute(change_bf, AXES, order_pairs())
    closing = call(closing_kernel, arr(shard, BF), None, (start, earlier, change), (size, 8 * size))
    return applied(closing, queries, gain)


def solution(mesh):
    rows = P(AXES, None)
    return jax.shard_map(
        shards,
        mesh=mesh,
        in_specs=(rows, rows, rows, P(AXES), P(), P()),
        out_specs=rows,
        check_vma=False,
    )
```

```python
import functools
import itertools

import jax
import jax.numpy as jnp
from jax import lax
from jax.experimental import pallas as pl
from jax.experimental.pallas import tpu as pltpu
from jax.sharding import PartitionSpec as P

SIDE = 4
AXES = ("order", "tok")
BF = jnp.bfloat16
F32 = jnp.float32
NT = (((1,), (1,)), ((), ()))
NN = (((1,), (0,)), ((), ()))
VMEM = pl.BlockSpec(memory_space=pltpu.VMEM)
SMEM = pl.BlockSpec(memory_space=pltpu.SMEM)


def flat(core, z, y, x):
    return ((core * SIDE + z % SIDE) * SIDE + y % SIDE) * SIDE + x % SIDE


def hop_pairs(level, step):
    pairs = []
    for core, z, y, x in itertools.product(range(2), *[range(SIDE)] * 3):
        dz = dy = dx = 0
        if level == 2:
            dz = step
        elif (level == 0) == (core == 0):
            dx = step
        else:
            dy = step
        pairs.append((flat(core, z, y, x), flat(core, z + dz, y + dy, x + dx)))
    return pairs


def hop(x, level, step):
    return lax.ppermute(x, AXES, hop_pairs(level, step % SIDE))


HBM = pl.BlockSpec(memory_space=pltpu.HBM)


def call(
    kernel, outs, specs, args, cost, scratch=(), out_spec=VMEM, limit=24 << 20, aliases={}
):
    return pl.pallas_call(
        kernel,
        out_shape=outs,
        in_specs=specs or [VMEM] * len(args),
        out_specs=jax.tree.map(lambda _: out_spec, outs),
        scratch_shapes=scratch,
        input_output_aliases=aliases,
        compiler_params=pltpu.CompilerParams(vmem_limit_bytes=limit),
        cost_estimate=pl.CostEstimate(flops=cost[0], bytes_accessed=cost[1], transcendentals=0),
    )(*args)


def arr(shape, dtype):
    return jax.ShapeDtypeStruct(shape, dtype)


def first_kernel(factor, tile, place, *refs):
    sources, outs, scratch = refs[:4], refs[4:12], refs[12:]
    k_ref, v_ref, rate_ref, b0, b1, b3, own, g2 = outs
    w_ref, turned, slab, b2, grads, hiddens, sems = scratch
    copies = []
    for src, dst in zip(sources, (w_ref, k_ref, v_ref, rate_ref)):
        count = sems.shape[1] if src.shape[0] > 1 else 1
        rows = src.shape[0] // count
        for j in range(count):
            part = pl.ds(j * rows, rows)
            sem = sems.at[len(copies) // sems.shape[1], j]
            copies.append(pltpu.make_async_copy(src.at[part], dst.at[part], sem))
            copies[-1].start()
    width = w_ref.shape[0]
    lines = width // (SIDE * SIDE)
    rows = width // sems.shape[1]
    for j, copy in enumerate(copies[: sems.shape[1]]):
        copy.wait()
        part = slice(j * rows, (j + 1) * rows)
        for m in range(2):
            piece = w_ref[part, m * width : (m + 1) * width].astype(BF)
            turned[m, :, :, part] = piece.T.reshape(SIDE * SIDE, lines, rows)
        piece = w_ref[part, 2 * width :].astype(BF)
        turned[2, j * rows // lines : (j + 1) * rows // lines] = piece.reshape(-1, lines, width)
    for r, block in enumerate((b0, b1, b2, b3)):
        for s in range(SIDE):
            group = place[r * SIDE + s]
            for m in range(3):
                block[s, m] = turned[m, group]
    mine = place[0]
    for m in range(2):
        start = pl.multiple_of(m * width + (mine // SIDE) * 128, 128)
        slab[...] = w_ref[:, pl.ds(start, 128)].T.reshape(SIDE, lines, width)
        own[m] = slab[mine % SIDE]
    own[2] = w_ref[pl.ds(pl.multiple_of(mine * lines, lines), lines), 2 * width :]
    for copy in copies[sems.shape[1] :]:
        copy.wait()
    gradient_kernel(factor, tile, 1, b2, k_ref, v_ref, rate_ref, g2, grads, hiddens)


def rows_of(w_refs, m):
    parts = [w[:, m].reshape(-1, w.shape[3]) for w in w_refs]
    return parts[0] if len(parts) == 1 else jnp.concatenate(parts, axis=0)


def gradient_kernel(factor, tile, count, *refs):
    w_refs, (k_ref, v_ref, rate_ref) = refs[:count], refs[count : count + 3]
    outs, (grads, hiddens) = refs[count + 3 : 2 * count + 3], refs[2 * count + 3 :]
    wgu = jnp.concatenate([rows_of(w_refs, 0), rows_of(w_refs, 1)], axis=0)
    wd = rows_of(w_refs, 2)
    units, width = wd.shape
    for i in range(k_ref.shape[0] // tile):
        rows = slice(i * tile, (i + 1) * tile)
        scale = -(rate_ref[:, rows] * factor)
        gu = lax.dot_general(wgu, k_ref[rows, :], NT, preferred_element_type=F32)
        hidden_grad = lax.dot_general(wd, v_ref[rows, :], NT, preferred_element_type=F32) * scale
        gate = gu[:units]
        up = gu[units:]
        sig = 0.5 * jnp.tanh(0.5 * gate) + 0.5
        act = gate * sig
        hiddens[:, rows] = (act * up * scale).astype(BF)
        grads[:units, rows] = (hidden_grad * up * (sig + act * (1.0 - sig))).astype(BF)
        grads[units:, rows] = (hidden_grad * act).astype(BF)
    upper = lax.dot_general(grads[...], k_ref[...], NN, preferred_element_type=F32)
    lower = lax.dot_general(hiddens[...], v_ref[...], NN, preferred_element_type=F32)
    lines = outs[0].shape[2]
    per = units // count
    for b, out in enumerate(outs):
        own = slice(b * per, (b + 1) * per)
        for m, part in enumerate((upper[:units], upper[units:], lower)):
            out[:, m] = part[own].reshape(SIDE, lines, width).astype(out.dtype)


def gradient_blocks(weights, keys, values, rates, factor, dtype, tile=256):
    count = len(weights)
    units = count * weights[0].shape[0] * weights[0].shape[2]
    tokens, width = keys.shape
    return call(
        functools.partial(gradient_kernel, factor, tile, count),
        [arr(w.shape, dtype) for w in weights],
        None,
        (*weights, keys, values, rates),
        (12 * tokens * width * units, 4 * tokens * width),
        [pltpu.VMEM((2 * units, tokens), BF), pltpu.VMEM((units, tokens), BF)],
    )


def far_kernel(own, r2, out):
    out[...] = own[...] + r2[...].astype(F32)


def scatter_kernel(far, r1, r3, keep, s1, s2, s3):
    for s, out in enumerate((keep, s1, s2, s3)):
        out[...] = (far[s] + r1[s].astype(F32) + r3[s].astype(F32)).astype(out.dtype)


def total_of(own, r1, r2, r3):
    return (own[...].astype(F32) + r1[...].astype(F32)) + (r2[...].astype(F32) + r3[...].astype(F32))


def add_kernel(own, r1, r2, r3, out):
    out[...] = total_of(own, r1, r2, r3).astype(out.dtype)


def update_kernel(weights, own, r1, r2, r3, new, new_bf):
    value = weights[...] - total_of(own, r1, r2, r3)
    new[...] = value
    new_bf[...] = value.astype(BF)


def change_kernel(start, weights, own, r1, r2, r3, change, change_bf):
    value = (weights[...] - total_of(own, r1, r2, r3)) - start[...]
    change[...] = value
    change_bf[...] = value.astype(BF)


def closing_kernel(group, start, other, change, out):
    earlier = jnp.where(group[0] > 0, other[...].astype(F32), 0.0)
    out[...] = ((start[...] + earlier) + change[...]).astype(BF)


def join_all_kernel(own, r1, r2, r3, out):
    for s, part in enumerate((own, r1, r2, r3)):
        out[s] = part[...]


def join_first_kernel(own, part, out, token):
    out[0] = own[...]
    out[1] = part[...]
    token[...] = own[0, : token.shape[0], : token.shape[1]]


def join_kernel(slot, joined, part, *rest):
    rest[-1][slot] = part[...]


def apply_kernel(tile, count, first, last, *refs):
    refs = list(refs)
    w_refs, q_ref = refs[:count], refs[count]
    refs = refs[count + 1 :]
    gain = refs.pop(0) if last else None
    so_far = None if first else refs.pop(0)
    out = refs.pop(0)
    wgu = jnp.concatenate([rows_of(w_refs, 0), rows_of(w_refs, 1)], axis=0)
    wd = rows_of(w_refs, 2)
    units = wd.shape[0]
    copies = []
    for i in range(q_ref.shape[0] // tile):
        rows = slice(i * tile, (i + 1) * tile)
        gu = lax.dot_general(q_ref[rows, :], wgu, NT, preferred_element_type=F32)
        gate = gu[:, :units]
        up = gu[:, units:]
        act = gate * (0.5 * jnp.tanh(0.5 * gate) + 0.5)
        y = lax.dot_general((act * up).astype(BF), wd, NN, preferred_element_type=F32)
        if so_far is not None:
            y = y + so_far[rows, :]
        if last:
            held, sems = refs
            scale = lax.rsqrt(jnp.mean(y * y, axis=1, keepdims=True) + 1e-06)
            held[rows, :] = (y * scale * gain[...]).astype(BF)
            copies.append(pltpu.make_async_copy(held.at[rows], out.at[rows], sems.at[i]))
            copies[-1].start()
        else:
            out[rows, :] = y
    for copy in copies:
        copy.wait()


def apply_blocks(weights, queries, so_far, gain, tile=512):
    count = len(weights)
    units = count * weights[0].shape[0] * weights[0].shape[2]
    tokens, width = queries.shape
    first, last = so_far is None, gain is not None
    args = (*weights, queries) + ((gain,) if last else ()) + (() if first else (so_far,))
    scratch = ()
    if last:
        scratch = [pltpu.VMEM((tokens, width), BF), pltpu.SemaphoreType.DMA((tokens // tile,))]
    return call(
        functools.partial(apply_kernel, tile, count, first, last),
        arr((tokens, width), BF if last else F32),
        None,
        args,
        (6 * tokens * width * units, 6 * tokens * width),
        scratch,
        out_spec=HBM if last else VMEM,
    )


def in_turn(first, *later):
    return lax.optimization_barrier((first, *later))


def ring_parts(x, level):
    return [hop(x, level, -r) for r in range(1, SIDE)]


def combined(own, sent):
    shard = own.shape[1:]
    size = own.size
    far = call(far_kernel, arr(own.shape, F32), None, (own, sent[2]), (size, 10 * size))
    keep, *out = call(
        scatter_kernel,
        [arr(shard, F32)] + [arr(shard, BF)] * 3,
        None,
        (far, sent[1], sent[3]),
        (2 * size, 10 * size),
    )
    got = [hop(x, 1, r + 1) for r, x in enumerate(out)]
    part = call(add_kernel, arr(shard, BF), None, (keep, *got), (size, 3 * size))
    return [part] + ring_parts(part, 2)


def first_totals(place, weights, keys, values, rates, factor, tile=256):
    sources = (weights, keys, values, rates)
    tokens, width = keys.shape
    lines = width // (SIDE * SIDE)
    block = (SIDE, 3, lines, width)
    units = SIDE * lines
    keys, values, rates, b0, b1, b3, start, g2 = call(
        functools.partial(first_kernel, factor, tile),
        [arr(keys.shape, BF), arr(values.shape, BF), arr(rates.shape, F32)]
        + [arr(block, BF)] * 3
        + [arr(block[1:], F32), arr(block, BF)],
        [SMEM] + [HBM] * 4,
        (place, *(pltpu.with_memory_space_constraint(x, pltpu.HBM) for x in sources)),
        (12 * tokens * width * units, 4 * tokens * width),
        [
            pltpu.VMEM(weights.shape, F32),
            pltpu.VMEM((3, SIDE * SIDE, lines, width), BF),
            pltpu.VMEM((SIDE, lines, width), F32),
            pltpu.VMEM(block, BF),
            pltpu.VMEM((2 * units, tokens), BF),
            pltpu.VMEM((units, tokens), BF),
            pltpu.SemaphoreType.DMA((4, 4)),
        ],
        limit=32 << 20,
    )
    sent = {2: hop(g2, 0, 2)}
    g1, g3 = gradient_blocks([b1, b3], keys, values, rates, factor, BF)
    sent[1], sent[3] = hop(g1, 0, 1), hop(g3, 0, 3)
    (own,) = gradient_blocks([b0], keys, values, rates, factor, F32)
    return start, (keys, values, rates), combined(own, sent)


def order_pairs():
    places = list(itertools.product(range(2), *[range(SIDE)] * 3))
    return [(flat(core, *c), flat(1 - core, *c)) for core, *c in places]


def gathered(shard, in_step):
    parts = ring_parts(shard, 1)
    block = arr((SIDE, *shard.shape), BF)
    cost = (0, 4 * shard.size)
    if not in_step:
        return call(join_all_kernel, block, None, (shard, *parts), cost)
    outs = [block, arr((16, 128), BF)]
    joined, token = call(join_first_kernel, outs, None, (shard, parts[0]), cost)
    more = [[], [lax.ppermute(token, AXES, order_pairs())]]
    for r in (2, 3):
        kernel = functools.partial(join_kernel, r)
        args = (joined, parts[r - 1], *more[r - 2])
        joined = call(kernel, block, None, args, cost, aliases={0: 0})
    return joined


def second_totals(shard, keys, values, rates, factor):
    block = gathered(shard, True)
    b2, b1, b3 = hop(block, 0, -2), hop(block, 0, -1), hop(block, 0, -3)
    (own,) = gradient_blocks([block], keys, values, rates, factor, F32)
    own, keys = in_turn(own, keys)
    (g2,) = gradient_blocks([b2], keys, values, rates, factor, BF)
    sent = {2: hop(g2, 0, 2)}
    g2, keys = in_turn(g2, keys)
    g1, g3 = gradient_blocks([b1, b3], keys, values, rates, factor, BF)
    sent[1], sent[3] = hop(g1, 0, 1), hop(g3, 0, 3)
    return combined(own, sent)


def applied(shard, queries, gain):
    block = gathered(shard, False)
    b2, b1, b3 = hop(block, 0, -2), hop(block, 0, -1), hop(block, 0, -3)
    result = apply_blocks([block], queries, None, None)
    result = apply_blocks([b2], queries, result, None)
    return apply_blocks([b1, b3], queries, result, gain)


def shards(queries, key_tokens, value_tokens, learn_rates, fast_init, out_gain):
    tokens, width = key_tokens.shape
    factor = (tokens * lax.axis_size("tok")) ** (-0.5)
    core = lax.axis_index("order")
    tok = lax.axis_index("tok")
    x, y = tok % SIDE, (tok // SIDE) % SIDE
    ring = jnp.arange(SIDE, dtype=jnp.int32)
    r1, r2 = ring[:, None], ring[None, :]
    along_x = (x + jnp.where(core == 0, r1, r2)) % SIDE
    along_y = (y + jnp.where(core == 0, r2, r1)) % SIDE
    place = (along_x * SIDE + along_y).reshape(-1).astype(jnp.int32)
    rates = learn_rates.reshape(1, tokens)
    gain = out_gain.reshape(1, width)

    start, tokens_in, parts = first_totals(place, fast_init, key_tokens, value_tokens, rates, factor)
    shard = start.shape
    size = start.size
    first_step, shard_bf = call(
        update_kernel, [arr(shard, F32), arr(shard, BF)], None, (start, *parts), (size, 8 * size)
    )
    parts = second_totals(shard_bf, *tokens_in, factor)
    change, change_bf = call(
        change_kernel,
        [arr(shard, F32), arr(shard, BF)],
        None,
        (start, first_step, *parts),
        (size, 8 * size),
    )
    other = lax.ppermute(change_bf, AXES, order_pairs())
    group = core.reshape(1).astype(jnp.int32)
    closing = call(
        closing_kernel,
        arr(shard, BF),
        [SMEM] + [VMEM] * 3,
        (group, start, other, change),
        (size, 8 * size),
    )
    return applied(closing, queries, gain)


def solution(mesh):
    rows = P(AXES, None)
    return jax.shard_map(
        shards,
        mesh=mesh,
        in_specs=(rows, rows, rows, P(AXES), P(), P()),
        out_specs=rows,
        check_vma=False,
    )
```

```python
import functools
import itertools

import jax
import jax.numpy as jnp
from jax import lax
from jax.experimental import pallas as pl
from jax.experimental.pallas import tpu as pltpu
from jax.sharding import PartitionSpec as P

SIDE = 4
AXES = ("order", "tok")
BF = jnp.bfloat16
F32 = jnp.float32
NT = (((1,), (1,)), ((), ()))
NN = (((1,), (0,)), ((), ()))
VMEM = pl.BlockSpec(memory_space=pltpu.VMEM)
SMEM = pl.BlockSpec(memory_space=pltpu.SMEM)


def flat(core, z, y, x):
    return ((core * SIDE + z % SIDE) * SIDE + y % SIDE) * SIDE + x % SIDE


def hop_pairs(level, step):
    pairs = []
    for core, z, y, x in itertools.product(range(2), *[range(SIDE)] * 3):
        dz = dy = dx = 0
        if level == 2:
            dz = step
        elif (level == 0) == (core == 0):
            dx = step
        else:
            dy = step
        pairs.append((flat(core, z, y, x), flat(core, z + dz, y + dy, x + dx)))
    return pairs


def hop(x, level, step):
    return lax.ppermute(x, AXES, hop_pairs(level, step % SIDE))


HBM = pl.BlockSpec(memory_space=pltpu.HBM)


def call(
    kernel, outs, specs, args, cost, scratch=(), out_spec=VMEM, limit=24 << 20, aliases={}
):
    return pl.pallas_call(
        kernel,
        out_shape=outs,
        in_specs=specs or [VMEM] * len(args),
        out_specs=jax.tree.map(lambda _: out_spec, outs),
        scratch_shapes=scratch,
        input_output_aliases=aliases,
        compiler_params=pltpu.CompilerParams(vmem_limit_bytes=limit),
        cost_estimate=pl.CostEstimate(flops=cost[0], bytes_accessed=cost[1], transcendentals=0),
    )(*args)


def arr(shape, dtype):
    return jax.ShapeDtypeStruct(shape, dtype)


def first_kernel(factor, tile, place, *refs):
    sources, outs, scratch = refs[:4], refs[4:12], refs[12:]
    k_ref, v_ref, rate_ref, b0, b1, b3, own, g2 = outs
    w_ref, turned, slab, b2, grads, hiddens, sems = scratch
    copies = []
    for src, dst in zip(sources, (w_ref, k_ref, v_ref, rate_ref)):
        count = sems.shape[1] if src.shape[0] > 1 else 1
        rows = src.shape[0] // count
        for j in range(count):
            part = pl.ds(j * rows, rows)
            sem = sems.at[len(copies) // sems.shape[1], j]
            copies.append(pltpu.make_async_copy(src.at[part], dst.at[part], sem))
            copies[-1].start()
    width = w_ref.shape[0]
    lines = width // (SIDE * SIDE)
    rows = width // sems.shape[1]
    for j, copy in enumerate(copies[: sems.shape[1]]):
        copy.wait()
        part = slice(j * rows, (j + 1) * rows)
        for m in range(2):
            piece = w_ref[part, m * width : (m + 1) * width].astype(BF)
            turned[m, :, :, part] = piece.T.reshape(SIDE * SIDE, lines, rows)
        piece = w_ref[part, 2 * width :].astype(BF)
        turned[2, j * rows // lines : (j + 1) * rows // lines] = piece.reshape(-1, lines, width)
    for r, block in enumerate((b0, b1, b2, b3)):
        for s in range(SIDE):
            group = place[r * SIDE + s]
            for m in range(3):
                block[s, m] = turned[m, group]
    mine = place[0]
    for m in range(2):
        start = pl.multiple_of(m * width + (mine // SIDE) * 128, 128)
        slab[...] = w_ref[:, pl.ds(start, 128)].T.reshape(SIDE, lines, width)
        own[m] = slab[mine % SIDE]
    own[2] = w_ref[pl.ds(pl.multiple_of(mine * lines, lines), lines), 2 * width :]
    for copy in copies[sems.shape[1] :]:
        copy.wait()
    gradient_kernel(factor, tile, 1, b2, k_ref, v_ref, rate_ref, g2, grads, hiddens)


def rows_of(w_refs, m):
    parts = [w[:, m].reshape(-1, w.shape[3]) for w in w_refs]
    return parts[0] if len(parts) == 1 else jnp.concatenate(parts, axis=0)


def gradient_kernel(factor, tile, count, *refs):
    w_refs, (k_ref, v_ref, rate_ref) = refs[:count], refs[count : count + 3]
    outs, (grads, hiddens) = refs[count + 3 : 2 * count + 3], refs[2 * count + 3 :]
    wgu = jnp.concatenate([rows_of(w_refs, 0), rows_of(w_refs, 1)], axis=0)
    wd = rows_of(w_refs, 2)
    units, width = wd.shape
    for i in range(k_ref.shape[0] // tile):
        rows = slice(i * tile, (i + 1) * tile)
        scale = -(rate_ref[:, rows] * factor)
        gu = lax.dot_general(wgu, k_ref[rows, :], NT, preferred_element_type=F32)
        hidden_grad = lax.dot_general(wd, v_ref[rows, :], NT, preferred_element_type=F32) * scale
        gate = gu[:units]
        up = gu[units:]
        sig = 0.5 * jnp.tanh(0.5 * gate) + 0.5
        act = gate * sig
        hiddens[:, rows] = (act * up * scale).astype(BF)
        grads[:units, rows] = (hidden_grad * up * (sig + act * (1.0 - sig))).astype(BF)
        grads[units:, rows] = (hidden_grad * act).astype(BF)
    upper = lax.dot_general(grads[...], k_ref[...], NN, preferred_element_type=F32)
    lower = lax.dot_general(hiddens[...], v_ref[...], NN, preferred_element_type=F32)
    lines = outs[0].shape[2]
    per = units // count
    for b, out in enumerate(outs):
        own = slice(b * per, (b + 1) * per)
        for m, part in enumerate((upper[:units], upper[units:], lower)):
            out[:, m] = part[own].reshape(SIDE, lines, width).astype(out.dtype)


def gradient_blocks(weights, keys, values, rates, factor, dtype, tile=256):
    count = len(weights)
    units = count * weights[0].shape[0] * weights[0].shape[2]
    tokens, width = keys.shape
    return call(
        functools.partial(gradient_kernel, factor, tile, count),
        [arr(w.shape, dtype) for w in weights],
        None,
        (*weights, keys, values, rates),
        (12 * tokens * width * units, 4 * tokens * width),
        [pltpu.VMEM((2 * units, tokens), BF), pltpu.VMEM((units, tokens), BF)],
    )


def far_kernel(own, r2, out):
    out[...] = own[...] + r2[...].astype(F32)


def scatter_kernel(far, r1, r3, keep, s1, s2, s3):
    for s, out in enumerate((keep, s1, s2, s3)):
        out[...] = (far[s] + r1[s].astype(F32) + r3[s].astype(F32)).astype(out.dtype)


def total_of(own, r1, r2, r3):
    return (own[...].astype(F32) + r1[...].astype(F32)) + (r2[...].astype(F32) + r3[...].astype(F32))


def add_kernel(own, r1, r2, r3, out):
    out[...] = total_of(own, r1, r2, r3).astype(out.dtype)


def update_kernel(weights, own, r1, r2, r3, new, new_bf):
    value = weights[...] - total_of(own, r1, r2, r3)
    new[...] = value
    new_bf[...] = value.astype(BF)


def change_kernel(start, weights, own, r1, r2, r3, change, change_bf):
    value = (weights[...] - total_of(own, r1, r2, r3)) - start[...]
    change[...] = value
    change_bf[...] = value.astype(BF)


def closing_kernel(group, start, other, change, out):
    earlier = jnp.where(group[0] > 0, other[...].astype(F32), 0.0)
    out[...] = ((start[...] + earlier) + change[...]).astype(BF)


def join_all_kernel(own, r1, r2, r3, out):
    for s, part in enumerate((own, r1, r2, r3)):
        out[s] = part[...]


def join_first_kernel(own, part, out, token):
    out[0] = own[...]
    out[1] = part[...]
    token[...] = own[0, : token.shape[0], : token.shape[1]]


def join_kernel(slot, joined, part, *rest):
    rest[-1][slot] = part[...]


def apply_kernel(tile, count, first, last, *refs):
    refs = list(refs)
    w_refs, q_ref = refs[:count], refs[count]
    refs = refs[count + 1 :]
    gain = refs.pop(0) if last else None
    so_far = None if first else refs.pop(0)
    out = refs.pop(0)
    wgu = jnp.concatenate([rows_of(w_refs, 0), rows_of(w_refs, 1)], axis=0)
    wd = rows_of(w_refs, 2)
    units = wd.shape[0]
    copies = []
    for i in range(q_ref.shape[0] // tile):
        rows = slice(i * tile, (i + 1) * tile)
        gu = lax.dot_general(q_ref[rows, :], wgu, NT, preferred_element_type=F32)
        gate = gu[:, :units]
        up = gu[:, units:]
        act = gate * (0.5 * jnp.tanh(0.5 * gate) + 0.5)
        y = lax.dot_general((act * up).astype(BF), wd, NN, preferred_element_type=F32)
        if so_far is not None:
            y = y + so_far[rows, :]
        if last:
            held, sems = refs
            scale = lax.rsqrt(jnp.mean(y * y, axis=1, keepdims=True) + 1e-06)
            held[rows, :] = (y * scale * gain[...]).astype(BF)
            copies.append(pltpu.make_async_copy(held.at[rows], out.at[rows], sems.at[i]))
            copies[-1].start()
        else:
            out[rows, :] = y
    for copy in copies:
        copy.wait()


def apply_blocks(weights, queries, so_far, gain, tile=512):
    count = len(weights)
    units = count * weights[0].shape[0] * weights[0].shape[2]
    tokens, width = queries.shape
    first, last = so_far is None, gain is not None
    args = (*weights, queries) + ((gain,) if last else ()) + (() if first else (so_far,))
    scratch = ()
    if last:
        scratch = [pltpu.VMEM((tokens, width), BF), pltpu.SemaphoreType.DMA((tokens // tile,))]
    return call(
        functools.partial(apply_kernel, tile, count, first, last),
        arr((tokens, width), BF if last else F32),
        None,
        args,
        (6 * tokens * width * units, 6 * tokens * width),
        scratch,
        out_spec=HBM if last else VMEM,
    )


def in_turn(first, *later):
    return lax.optimization_barrier((first, *later))


def ring_parts(x, level):
    return [hop(x, level, -r) for r in range(1, SIDE)]


def combined(own, sent):
    shard = own.shape[1:]
    size = own.size
    far = call(far_kernel, arr(own.shape, F32), None, (own, sent[2]), (size, 10 * size))
    keep, *out = call(
        scatter_kernel,
        [arr(shard, F32)] + [arr(shard, BF)] * 3,
        None,
        (far, sent[1], sent[3]),
        (2 * size, 10 * size),
    )
    got = [hop(x, 1, r + 1) for r, x in enumerate(out)]
    part = call(add_kernel, arr(shard, BF), None, (keep, *got), (size, 3 * size))
    return [part] + ring_parts(part, 2)


def first_totals(place, weights, keys, values, rates, factor, tile=256):
    sources = (weights, keys, values, rates)
    tokens, width = keys.shape
    lines = width // (SIDE * SIDE)
    block = (SIDE, 3, lines, width)
    units = SIDE * lines
    keys, values, rates, b0, b1, b3, start, g2 = call(
        functools.partial(first_kernel, factor, tile),
        [arr(keys.shape, BF), arr(values.shape, BF), arr(rates.shape, F32)]
        + [arr(block, BF)] * 3
        + [arr(block[1:], F32), arr(block, BF)],
        [SMEM] + [HBM] * 4,
        (place, *(pltpu.with_memory_space_constraint(x, pltpu.HBM) for x in sources)),
        (12 * tokens * width * units, 4 * tokens * width),
        [
            pltpu.VMEM(weights.shape, F32),
            pltpu.VMEM((3, SIDE * SIDE, lines, width), BF),
            pltpu.VMEM((SIDE, lines, width), F32),
            pltpu.VMEM(block, BF),
            pltpu.VMEM((2 * units, tokens), BF),
            pltpu.VMEM((units, tokens), BF),
            pltpu.SemaphoreType.DMA((4, 4)),
        ],
        limit=32 << 20,
    )
    sent = {2: hop(g2, 0, 2)}
    g1, g3 = gradient_blocks([b1, b3], keys, values, rates, factor, BF)
    sent[1], sent[3] = hop(g1, 0, 1), hop(g3, 0, 3)
    (own,) = gradient_blocks([b0], keys, values, rates, factor, F32)
    return start, (keys, values, rates), combined(own, sent)


def order_pairs():
    places = list(itertools.product(range(2), *[range(SIDE)] * 3))
    return [(flat(core, *c), flat(1 - core, *c)) for core, *c in places]


def gathered(shard, in_step):
    parts = ring_parts(shard, 1)
    block = arr((SIDE, *shard.shape), BF)
    cost = (0, 4 * shard.size)
    if not in_step:
        return call(join_all_kernel, block, None, (shard, *parts), cost)
    outs = [block, arr((16, 128), BF)]
    joined, token = call(join_first_kernel, outs, None, (shard, parts[0]), cost)
    more = [[], [lax.ppermute(token, AXES, order_pairs())]]
    for r in (2, 3):
        kernel = functools.partial(join_kernel, r)
        args = (joined, parts[r - 1], *more[r - 2])
        joined = call(kernel, block, None, args, cost, aliases={0: 0})
    return joined


def second_totals(shard, keys, values, rates, factor):
    block = gathered(shard, True)
    b2, b1, b3 = hop(block, 0, -2), hop(block, 0, -1), hop(block, 0, -3)
    (own,) = gradient_blocks([block], keys, values, rates, factor, F32)
    own, keys = in_turn(own, keys)
    (g2,) = gradient_blocks([b2], keys, values, rates, factor, BF)
    sent = {2: hop(g2, 0, 2)}
    g2, keys = in_turn(g2, keys)
    g1, g3 = gradient_blocks([b1, b3], keys, values, rates, factor, BF)
    sent[1], sent[3] = hop(g1, 0, 1), hop(g3, 0, 3)
    return combined(own, sent)


def applied(shard, queries, gain):
    block = gathered(shard, True)
    b2, b1, b3 = hop(block, 0, -2), hop(block, 0, -1), hop(block, 0, -3)
    result = apply_blocks([block], queries, None, None)
    result = apply_blocks([b2], queries, result, None)
    return apply_blocks([b1, b3], queries, result, gain)


def shards(queries, key_tokens, value_tokens, learn_rates, fast_init, out_gain):
    tokens, width = key_tokens.shape
    factor = (tokens * lax.axis_size("tok")) ** (-0.5)
    core = lax.axis_index("order")
    tok = lax.axis_index("tok")
    x, y = tok % SIDE, (tok // SIDE) % SIDE
    ring = jnp.arange(SIDE, dtype=jnp.int32)
    r1, r2 = ring[:, None], ring[None, :]
    along_x = (x + jnp.where(core == 0, r1, r2)) % SIDE
    along_y = (y + jnp.where(core == 0, r2, r1)) % SIDE
    place = (along_x * SIDE + along_y).reshape(-1).astype(jnp.int32)
    rates = learn_rates.reshape(1, tokens)
    gain = out_gain.reshape(1, width)

    start, tokens_in, parts = first_totals(place, fast_init, key_tokens, value_tokens, rates, factor)
    shard = start.shape
    size = start.size
    first_step, shard_bf = call(
        update_kernel, [arr(shard, F32), arr(shard, BF)], None, (start, *parts), (size, 8 * size)
    )
    parts = second_totals(shard_bf, *tokens_in, factor)
    change, change_bf = call(
        change_kernel,
        [arr(shard, F32), arr(shard, BF)],
        None,
        (start, first_step, *parts),
        (size, 8 * size),
    )
    other = lax.ppermute(change_bf, AXES, order_pairs())
    group = core.reshape(1).astype(jnp.int32)
    closing = call(
        closing_kernel,
        arr(shard, BF),
        [SMEM] + [VMEM] * 3,
        (group, start, other, change),
        (size, 8 * size),
    )
    return applied(closing, queries, gain)


def solution(mesh):
    rows = P(AXES, None)
    return jax.shard_map(
        shards,
        mesh=mesh,
        in_specs=(rows, rows, rows, P(AXES), P(), P()),
        out_specs=rows,
        check_vma=False,
    )
```

```python
import functools
import itertools

import jax
import jax.numpy as jnp
from jax import lax
from jax.experimental import pallas as pl
from jax.experimental.pallas import tpu as pltpu
from jax.sharding import PartitionSpec as P

SIDE = 4
AXES = ("order", "tok")
BF = jnp.bfloat16
F32 = jnp.float32
NT = (((1,), (1,)), ((), ()))
NN = (((1,), (0,)), ((), ()))
VMEM = pl.BlockSpec(memory_space=pltpu.VMEM)
SMEM = pl.BlockSpec(memory_space=pltpu.SMEM)


def flat(core, z, y, x):
    return ((core * SIDE + z % SIDE) * SIDE + y % SIDE) * SIDE + x % SIDE


def hop_pairs(level, step):
    pairs = []
    for core, z, y, x in itertools.product(range(2), *[range(SIDE)] * 3):
        dz = dy = dx = 0
        if level == 2:
            dz = step
        elif (level == 0) == (core == 0):
            dx = step
        else:
            dy = step
        pairs.append((flat(core, z, y, x), flat(core, z + dz, y + dy, x + dx)))
    return pairs


def hop(x, level, step):
    return lax.ppermute(x, AXES, hop_pairs(level, step % SIDE))


HBM = pl.BlockSpec(memory_space=pltpu.HBM)


def call(
    kernel, outs, specs, args, cost, scratch=(), out_spec=VMEM, limit=24 << 20, aliases={}
):
    return pl.pallas_call(
        kernel,
        out_shape=outs,
        in_specs=specs or [VMEM] * len(args),
        out_specs=jax.tree.map(lambda _: out_spec, outs),
        scratch_shapes=scratch,
        input_output_aliases=aliases,
        compiler_params=pltpu.CompilerParams(vmem_limit_bytes=limit),
        cost_estimate=pl.CostEstimate(flops=cost[0], bytes_accessed=cost[1], transcendentals=0),
    )(*args)


def arr(shape, dtype):
    return jax.ShapeDtypeStruct(shape, dtype)


def first_kernel(factor, tile, place, *refs):
    sources, outs, scratch = refs[:4], refs[4:12], refs[12:]
    k_ref, v_ref, rate_ref, b0, b1, b3, own, g2 = outs
    w_ref, turned, slab, b2, grads, hiddens, sems = scratch
    copies = []
    for src, dst in zip(sources, (w_ref, k_ref, v_ref, rate_ref)):
        count = sems.shape[1] if src.shape[0] > 1 else 1
        rows = src.shape[0] // count
        for j in range(count):
            part = pl.ds(j * rows, rows)
            sem = sems.at[len(copies) // sems.shape[1], j]
            copies.append(pltpu.make_async_copy(src.at[part], dst.at[part], sem))
    count = sems.shape[1]
    pairs = [copies[i * count + j] for j in range(count) for i in (1, 2)]
    for copy in (*copies[:count], copies[3 * count], *pairs):
        copy.start()
    width = w_ref.shape[0]
    lines = width // (SIDE * SIDE)
    rows = width // sems.shape[1]
    for j, copy in enumerate(copies[: sems.shape[1]]):
        copy.wait()
        part = slice(j * rows, (j + 1) * rows)
        for m in range(2):
            piece = w_ref[part, m * width : (m + 1) * width].astype(BF)
            turned[m, :, :, part] = piece.T.reshape(SIDE * SIDE, lines, rows)
        piece = w_ref[part, 2 * width :].astype(BF)
        turned[2, j * rows // lines : (j + 1) * rows // lines] = piece.reshape(-1, lines, width)
    for r, block in enumerate((b0, b1, b2, b3)):
        for s in range(SIDE):
            group = place[r * SIDE + s]
            for m in range(3):
                block[s, m] = turned[m, group]
    count = sems.shape[1]
    copies[3 * count].wait()

    def ready(i):
        tiles = k_ref.shape[0] // tile // count
        if i % tiles == 0:
            copies[count + i // tiles].wait()
            copies[2 * count + i // tiles].wait()

    refs = (b2, k_ref, v_ref, rate_ref, g2, grads, hiddens)
    gradient_kernel(factor, tile, 1, *refs, ready=ready)
    mine = place[0]
    for m in range(2):
        start = pl.multiple_of(m * width + (mine // SIDE) * 128, 128)
        slab[...] = w_ref[:, pl.ds(start, 128)].T.reshape(SIDE, lines, width)
        own[m] = slab[mine % SIDE]
    own[2] = w_ref[pl.ds(pl.multiple_of(mine * lines, lines), lines), 2 * width :]


def rows_of(w_refs, m):
    parts = [w[:, m].reshape(-1, w.shape[3]) for w in w_refs]
    return parts[0] if len(parts) == 1 else jnp.concatenate(parts, axis=0)


def gradient_kernel(factor, tile, count, *refs, ready=None):
    w_refs, (k_ref, v_ref, rate_ref) = refs[:count], refs[count : count + 3]
    outs, (grads, hiddens) = refs[count + 3 : 2 * count + 3], refs[2 * count + 3 :]
    wgu = jnp.concatenate([rows_of(w_refs, 0), rows_of(w_refs, 1)], axis=0)
    wd = rows_of(w_refs, 2)
    units, width = wd.shape
    for i in range(k_ref.shape[0] // tile):
        rows = slice(i * tile, (i + 1) * tile)
        if ready is not None:
            ready(i)
        scale = -(rate_ref[:, rows] * factor)
        gu = lax.dot_general(wgu, k_ref[rows, :], NT, preferred_element_type=F32)
        hidden_grad = lax.dot_general(wd, v_ref[rows, :], NT, preferred_element_type=F32) * scale
        gate = gu[:units]
        up = gu[units:]
        sig = 0.5 * jnp.tanh(0.5 * gate) + 0.5
        act = gate * sig
        hiddens[:, rows] = (act * up * scale).astype(BF)
        grads[:units, rows] = (hidden_grad * up * (sig + act * (1.0 - sig))).astype(BF)
        grads[units:, rows] = (hidden_grad * act).astype(BF)
    upper = lax.dot_general(grads[...], k_ref[...], NN, preferred_element_type=F32)
    lower = lax.dot_general(hiddens[...], v_ref[...], NN, preferred_element_type=F32)
    lines = outs[0].shape[2]
    per = units // count
    for b, out in enumerate(outs):
        own = slice(b * per, (b + 1) * per)
        for m, part in enumerate((upper[:units], upper[units:], lower)):
            out[:, m] = part[own].reshape(SIDE, lines, width).astype(out.dtype)


def gradient_blocks(weights, keys, values, rates, factor, dtype, tile=256):
    count = len(weights)
    units = count * weights[0].shape[0] * weights[0].shape[2]
    tokens, width = keys.shape
    return call(
        functools.partial(gradient_kernel, factor, tile, count),
        [arr(w.shape, dtype) for w in weights],
        None,
        (*weights, keys, values, rates),
        (12 * tokens * width * units, 4 * tokens * width),
        [pltpu.VMEM((2 * units, tokens), BF), pltpu.VMEM((units, tokens), BF)],
    )


def far_kernel(own, r2, out):
    out[...] = own[...] + r2[...].astype(F32)


def scatter_kernel(far, r1, r3, keep, s1, s2, s3):
    for s, out in enumerate((keep, s1, s2, s3)):
        out[...] = (far[s] + r1[s].astype(F32) + r3[s].astype(F32)).astype(out.dtype)


def total_of(own, r1, r2, r3):
    return (own[...].astype(F32) + r1[...].astype(F32)) + (r2[...].astype(F32) + r3[...].astype(F32))


def add_kernel(own, r1, r2, r3, out):
    out[...] = total_of(own, r1, r2, r3).astype(out.dtype)


def update_kernel(weights, own, r1, r2, r3, new, new_bf):
    value = weights[...] - total_of(own, r1, r2, r3)
    new[...] = value
    new_bf[...] = value.astype(BF)


def change_kernel(start, weights, own, r1, r2, r3, change, change_bf):
    value = (weights[...] - total_of(own, r1, r2, r3)) - start[...]
    change[...] = value
    change_bf[...] = value.astype(BF)


def closing_kernel(group, start, other, change, out):
    earlier = jnp.where(group[0] > 0, other[...].astype(F32), 0.0)
    out[...] = ((start[...] + earlier) + change[...]).astype(BF)


def join_all_kernel(own, r1, r2, r3, out):
    for s, part in enumerate((own, r1, r2, r3)):
        out[s] = part[...]


def join_first_kernel(own, part, out, token):
    out[0] = own[...]
    out[1] = part[...]
    token[...] = own[0, : token.shape[0], : token.shape[1]]


def join_kernel(slot, joined, part, *rest):
    rest[-1][slot] = part[...]


def apply_kernel(tile, count, first, last, *refs):
    refs = list(refs)
    w_refs, q_ref = refs[:count], refs[count]
    refs = refs[count + 1 :]
    gain = refs.pop(0) if last else None
    so_far = None if first else refs.pop(0)
    out = refs.pop(0)
    wgu = jnp.concatenate([rows_of(w_refs, 0), rows_of(w_refs, 1)], axis=0)
    wd = rows_of(w_refs, 2)
    units = wd.shape[0]
    copies = []
    for i in range(q_ref.shape[0] // tile):
        rows = slice(i * tile, (i + 1) * tile)
        gu = lax.dot_general(q_ref[rows, :], wgu, NT, preferred_element_type=F32)
        gate = gu[:, :units]
        up = gu[:, units:]
        act = gate * (0.5 * jnp.tanh(0.5 * gate) + 0.5)
        y = lax.dot_general((act * up).astype(BF), wd, NN, preferred_element_type=F32)
        if so_far is not None:
            y = y + so_far[rows, :]
        if last:
            held, sems = refs
            scale = lax.rsqrt(jnp.mean(y * y, axis=1, keepdims=True) + 1e-06)
            held[rows, :] = (y * scale * gain[...]).astype(BF)
            copies.append(pltpu.make_async_copy(held.at[rows], out.at[rows], sems.at[i]))
            copies[-1].start()
        else:
            out[rows, :] = y
    for copy in copies:
        copy.wait()


def apply_blocks(weights, queries, so_far, gain, tile=512):
    count = len(weights)
    units = count * weights[0].shape[0] * weights[0].shape[2]
    tokens, width = queries.shape
    first, last = so_far is None, gain is not None
    args = (*weights, queries) + ((gain,) if last else ()) + (() if first else (so_far,))
    scratch = ()
    if last:
        scratch = [pltpu.VMEM((tokens, width), BF), pltpu.SemaphoreType.DMA((tokens // tile,))]
    return call(
        functools.partial(apply_kernel, tile, count, first, last),
        arr((tokens, width), BF if last else F32),
        None,
        args,
        (6 * tokens * width * units, 6 * tokens * width),
        scratch,
        out_spec=HBM if last else VMEM,
    )


def in_turn(first, *later):
    return lax.optimization_barrier((first, *later))


def ring_parts(x, level):
    return [hop(x, level, -r) for r in range(1, SIDE)]


def combined(own, sent):
    shard = own.shape[1:]
    size = own.size
    far = call(far_kernel, arr(own.shape, F32), None, (own, sent[2]), (size, 10 * size))
    keep, *out = call(
        scatter_kernel,
        [arr(shard, F32)] + [arr(shard, BF)] * 3,
        None,
        (far, sent[1], sent[3]),
        (2 * size, 10 * size),
    )
    got = [hop(x, 1, r + 1) for r, x in enumerate(out)]
    part = call(add_kernel, arr(shard, BF), None, (keep, *got), (size, 3 * size))
    return [part] + ring_parts(part, 2)


def first_totals(place, weights, keys, values, rates, factor, tile=256):
    sources = (weights, keys, values, rates)
    tokens, width = keys.shape
    lines = width // (SIDE * SIDE)
    block = (SIDE, 3, lines, width)
    units = SIDE * lines
    keys, values, rates, b0, b1, b3, start, g2 = call(
        functools.partial(first_kernel, factor, tile),
        [arr(keys.shape, BF), arr(values.shape, BF), arr(rates.shape, F32)]
        + [arr(block, BF)] * 3
        + [arr(block[1:], F32), arr(block, BF)],
        [SMEM] + [HBM] * 4,
        (place, *(pltpu.with_memory_space_constraint(x, pltpu.HBM) for x in sources)),
        (12 * tokens * width * units, 4 * tokens * width),
        [
            pltpu.VMEM(weights.shape, F32),
            pltpu.VMEM((3, SIDE * SIDE, lines, width), BF),
            pltpu.VMEM((SIDE, lines, width), F32),
            pltpu.VMEM(block, BF),
            pltpu.VMEM((2 * units, tokens), BF),
            pltpu.VMEM((units, tokens), BF),
            pltpu.SemaphoreType.DMA((4, 4)),
        ],
        limit=32 << 20,
    )
    sent = {2: hop(g2, 0, 2)}
    g1, g3 = gradient_blocks([b1, b3], keys, values, rates, factor, BF)
    sent[1], sent[3] = hop(g1, 0, 1), hop(g3, 0, 3)
    (own,) = gradient_blocks([b0], keys, values, rates, factor, F32)
    return start, (keys, values, rates), combined(own, sent)


def order_pairs():
    places = list(itertools.product(range(2), *[range(SIDE)] * 3))
    return [(flat(core, *c), flat(1 - core, *c)) for core, *c in places]


def gathered(shard, in_step):
    parts = ring_parts(shard, 1)
    block = arr((SIDE, *shard.shape), BF)
    cost = (0, 4 * shard.size)
    if not in_step:
        return call(join_all_kernel, block, None, (shard, *parts), cost)
    outs = [block, arr((16, 128), BF)]
    joined, token = call(join_first_kernel, outs, None, (shard, parts[0]), cost)
    more = [[], [lax.ppermute(token, AXES, order_pairs())]]
    for r in (2, 3):
        kernel = functools.partial(join_kernel, r)
        args = (joined, parts[r - 1], *more[r - 2])
        joined = call(kernel, block, None, args, cost, aliases={0: 0})
    return joined


def second_totals(shard, keys, values, rates, factor):
    block = gathered(shard, True)
    b2, b1, b3 = hop(block, 0, -2), hop(block, 0, -1), hop(block, 0, -3)
    (own,) = gradient_blocks([block], keys, values, rates, factor, F32)
    own, keys = in_turn(own, keys)
    (g2,) = gradient_blocks([b2], keys, values, rates, factor, BF)
    sent = {2: hop(g2, 0, 2)}
    g2, keys = in_turn(g2, keys)
    g1, g3 = gradient_blocks([b1, b3], keys, values, rates, factor, BF)
    sent[1], sent[3] = hop(g1, 0, 1), hop(g3, 0, 3)
    return combined(own, sent)


def applied(shard, queries, gain):
    block = gathered(shard, True)
    b2, b1, b3 = hop(block, 0, -2), hop(block, 0, -1), hop(block, 0, -3)
    result = apply_blocks([block], queries, None, None)
    result = apply_blocks([b2], queries, result, None)
    return apply_blocks([b1, b3], queries, result, gain)


def shards(queries, key_tokens, value_tokens, learn_rates, fast_init, out_gain):
    tokens, width = key_tokens.shape
    factor = (tokens * lax.axis_size("tok")) ** (-0.5)
    core = lax.axis_index("order")
    tok = lax.axis_index("tok")
    x, y = tok % SIDE, (tok // SIDE) % SIDE
    ring = jnp.arange(SIDE, dtype=jnp.int32)
    r1, r2 = ring[:, None], ring[None, :]
    along_x = (x + jnp.where(core == 0, r1, r2)) % SIDE
    along_y = (y + jnp.where(core == 0, r2, r1)) % SIDE
    place = (along_x * SIDE + along_y).reshape(-1).astype(jnp.int32)
    rates = learn_rates.reshape(1, tokens)
    gain = out_gain.reshape(1, width)

    start, tokens_in, parts = first_totals(place, fast_init, key_tokens, value_tokens, rates, factor)
    shard = start.shape
    size = start.size
    first_step, shard_bf = call(
        update_kernel, [arr(shard, F32), arr(shard, BF)], None, (start, *parts), (size, 8 * size)
    )
    parts = second_totals(shard_bf, *tokens_in, factor)
    change, change_bf = call(
        change_kernel,
        [arr(shard, F32), arr(shard, BF)],
        None,
        (start, first_step, *parts),
        (size, 8 * size),
    )
    other = lax.ppermute(change_bf, AXES, order_pairs())
    group = core.reshape(1).astype(jnp.int32)
    closing = call(
        closing_kernel,
        arr(shard, BF),
        [SMEM] + [VMEM] * 3,
        (group, start, other, change),
        (size, 8 * size),
    )
    return applied(closing, queries, gain)


def solution(mesh):
    rows = P(AXES, None)
    return jax.shard_map(
        shards,
        mesh=mesh,
        in_specs=(rows, rows, rows, P(AXES), P(), P()),
        out_specs=rows,
        check_vma=False,
    )
```
